256 devices in a mesh: fluid: 64 (over z, x_hi, y), grp: 4 (over x_lo, core).
Axes of the slice: x: 4 (x_hi: 2, x_lo: 2; x = x_hi * 2 + x_lo), y: 4, z: 8, core: 2. Of those that a mesh axis runs over, the one named last changes fastest.
Arguments:
- acoustic_modes: bfloat16 [2097152, 400], P(('fluid', 'grp')), may hold values from -6 to 6
- shell_modes: bfloat16 [65536, 300], P('fluid'), may hold values from -0.0004272461 to 0.0004272461
- wet_counts: int32 [256], P(('fluid', 'grp')), may hold values from 1 to 2048, 209715 in all
- fluid_nodes: int32 [524288], P(('fluid', 'grp')), may hold values from 0 to 8191
- shell_nodes: int32 [524288], P(('fluid', 'grp')), may hold values from 0 to 1023
- wet_area: float32 [524288], P(('fluid', 'grp')), may hold values from 0.15 to 0.6
- shell_freq: float32 [300], replicated, may hold values from 1 to 2
- shell_loss: float32 [300], replicated, may hold values from 0.2 to 0.5
- cavity_freq: float32 [400], replicated, may hold values from 1 to 2
- cavity_loss: float32 [400], replicated, may hold values from 0.2 to 0.5
- freqs: float32 [64], replicated, may hold values from 0.7 to 2.2
- modal_force: float32 [300], replicated, may hold values from -1.5 to 1.5
- cavity_source: float32 [400], replicated, may hold values from -1.5 to 1.5
Outputs:
- pressure: bfloat16 [2097152, 128], P(('fluid', 'grp'))
- modal_structure: float32 [2, 64, 300], P(None, 'grp')
The draws below stay inside these ranges and needn't reach their ends.
Inputs may be any that keep to these rules, and one draw needn't show every extreme that they name: `wet_counts`: slots 0 to count - 1 of a device's 2048 interface slots are live, the others are ignored. `fluid_nodes`: numbered within the device's own 8192 cavity rows. `shell_nodes`: numbered within the 1024 shell rows of the device's fluid index.
All inputs are finite; a program needn't handle non-finite values.
Results may differ from the reference program's by a relative error of at most 0.0055.
Values may be sent and summed in bfloat16 or wider, within the bound.
A program may use at most 64 MiB of HBM per device.

```python
import math
import jax
import jax.numpy as jnp
import numpy as np
from jax import lax

MS = 300
MA = 400
F = 64
SECTIONS = 4
FD = 8192
SD = 1024
IF_MOST = 2048
FLUID_DOFS = 2097152
SHELL_DOFS = 65536
SLOTS = 524288
N_FLUID = 64
N_GRP = 4


def place_ends(entries, stream_key, smallest, high):
    extent = entries.shape
    spot = [jax.random.randint(jax.random.fold_in(stream_key, axis), (), 0, extent[axis]) for axis in range(len(extent))]
    entries = entries.at[tuple(spot)].set(smallest)
    longest = extent.index(max(extent))
    spot[longest] = (spot[longest] + 1) % extent[longest]
    return entries.at[tuple(spot)].set(high)


def steps_of(rng, shape, shards, smallest, top_value):
    def one(dim, parts):
        draws = jax.random.uniform(jax.random.fold_in(jax.random.fold_in(rng, 6), dim), (parts,), jnp.float32, smallest / len(shards), top_value / len(shards))
        return jnp.repeat(jnp.exp(draws), shape[dim] // parts).reshape((-1,) + (1,) * (len(shape) - dim - 1))

    level = one(*shards[0])
    for cut in shards[1:]:
        level = level * one(*cut)
    return level


def split_up(amount, total, limit, lean):
    weights = [(1 << 20) // math.isqrt(rank ** lean) + 1 for rank in range(2, amount + 1)]
    spare, counts = total - limit - (amount - 1), [1] * (amount - 1)
    while spare > 0:
        movable = [i for i in range(amount - 1) if counts[i] < limit]
        mass, budget = sum([weights[i] for i in movable]), spare
        for i in movable:
            addition = min(limit - counts[i], max(1, budget * weights[i] // mass), spare)
            counts[i] = counts[i] + addition
            spare = spare - addition
    return np.array([limit] + counts)


def ragged(own_key, number_of, total, most, lean):
    if number_of == 2:
        one = jax.random.randint(own_key, (), max(1, total - most), min(most, total - 1) + 1)
        return jnp.stack([one, total - one])
    sizes = jnp.asarray(split_up(number_of, total, most, lean), jnp.int32)
    twos = (number_of - 1) // 2
    donor, receiver = sizes[1:1 + 2 * twos:2], sizes[2:2 + 2 * twos:2]
    slack = jnp.minimum(donor - 1, most - receiver)
    passed = jax.random.randint(jax.random.fold_in(own_key, 1), (twos,), 0, 1 << 20) % (slack + 1)
    sizes = sizes.at[1:1 + 2 * twos:2].set(donor - passed).at[2:2 + 2 * twos:2].set(receiver + passed)
    return sizes[jax.random.permutation(jax.random.fold_in(own_key, 2), number_of)]


def centred(key, extent, scale, reach, split=(), held_as=jnp.bfloat16):
    entries = scale * jax.random.normal(key, extent, jnp.float32)
    if split:
        entries = entries * steps_of(key, extent, split, -0.22, 0.18)
    return jnp.clip(entries, -reach, reach).astype(held_as)


def setup_inputs(seed: int = 0) -> dict:
    splits = jax.random.split(jax.random.key(seed), 14)
    acoustic_modes = centred(splits[0], (FLUID_DOFS, MA), 1.0, 6.0, ((0, 256),))
    shell_modes = centred(splits[1], (SHELL_DOFS, MS), (N_FLUID * N_GRP * IF_MOST * MA) ** -0.5, 0.0004272461, ((0, 64),))
    wet_counts = ragged(splits[2], N_FLUID * N_GRP, N_FLUID * N_GRP * IF_MOST * 2 // 5, IF_MOST, 2).astype(jnp.int32)
    fluid_nodes = place_ends(jax.random.randint(splits[3], (SLOTS,), 0, FD), jax.random.fold_in(splits[3], 1), 0, FD - 1).astype(jnp.int32)
    shell_nodes = place_ends(jax.random.randint(splits[4], (SLOTS,), 0, SD), jax.random.fold_in(splits[4], 1), 0, SD - 1).astype(jnp.int32)
    wet_area = jnp.clip(jnp.exp(math.log(0.6) - 1.3862944 * jax.random.uniform(splits[5], (SLOTS,), jnp.float32) ** steps_of(splits[5], (SLOTS,), ((0, 256),), -0.2, 0.2)), 0.15, 0.6)
    shell_freq = jnp.clip(jnp.exp(jax.random.uniform(splits[6], (MS,), jnp.float32, math.log(1.0), math.log(2.0))), 1.0, 2.0)
    shell_loss = jnp.clip(jnp.exp(jax.random.uniform(splits[7], (MS,), jnp.float32, math.log(0.2), math.log(0.5))), 0.2, 0.5)
    cavity_freq = jnp.clip(jnp.exp(jax.random.uniform(splits[8], (MA,), jnp.float32, math.log(1.0), math.log(2.0))), 1.0, 2.0)
    cavity_loss = jnp.clip(jnp.exp(jax.random.uniform(splits[9], (MA,), jnp.float32, math.log(0.2), math.log(0.5))), 0.2, 0.5)
    freqs = jnp.clip(jax.random.uniform(splits[10], (F,), jnp.float32, 0.7, 2.2), 0.7, 2.2)
    modal_force = centred(splits[11], (MS,), 0.25, 1.5, (), jnp.float32)
    cavity_source = centred(splits[12], (MA,), 0.25, 1.5, (), jnp.float32)
    return dict(acoustic_modes=acoustic_modes, shell_modes=shell_modes, wet_counts=wet_counts, fluid_nodes=fluid_nodes, shell_nodes=shell_nodes, wet_area=wet_area, shell_freq=shell_freq, shell_loss=shell_loss, cavity_freq=cavity_freq, cavity_loss=cavity_loss, freqs=freqs, modal_force=modal_force, cavity_source=cavity_source)


HIGH = lax.Precision.HIGHEST


def divide_complex(real_part, imag_part, denom_real, denom_imag):
    scale = denom_real * denom_real + denom_imag * denom_imag
    return ((real_part * denom_real + imag_part * denom_imag) / scale,
            (imag_part * denom_real - real_part * denom_imag) / scale)


def modal_terms(omega, loss, freqs):
    stiff = omega * omega
    real_part = stiff[None, :] - (freqs * freqs)[:, None]
    imag_part = jnp.broadcast_to((loss * stiff)[None, :], real_part.shape)
    return real_part, imag_part


def reference(acoustic_modes, shell_modes, wet_counts, fluid_nodes, shell_nodes, wet_area, shell_freq, shell_loss, cavity_freq, cavity_loss, freqs, modal_force, cavity_source):
    devices = N_FLUID * N_GRP
    fluid_blocks = acoustic_modes.reshape(devices, FD, MA)
    shell_blocks = shell_modes.reshape(N_FLUID, SD, MS)

    def accumulate(carry, device):
        fluid_part = lax.dynamic_index_in_dim(fluid_blocks, device, 0, keepdims=False)
        shell_part = lax.dynamic_index_in_dim(shell_blocks, device // N_GRP, 0, keepdims=False)
        start = (device * IF_MOST).astype(jnp.int32)
        fluid_pick = lax.dynamic_slice_in_dim(fluid_nodes, start, IF_MOST)
        shell_pick = lax.dynamic_slice_in_dim(shell_nodes, start, IF_MOST)
        area = lax.dynamic_slice_in_dim(wet_area, start, IF_MOST)
        count = lax.dynamic_index_in_dim(wet_counts, device, 0, keepdims=False)
        live = (jnp.arange(IF_MOST, dtype=jnp.int32) < count).astype(jnp.float32)
        wet = (area[:, None] * fluid_part[fluid_pick].astype(jnp.float32) * live[:, None]).astype(jnp.bfloat16)
        shell_rows = shell_part[shell_pick]
        carry = carry + jnp.dot(shell_rows.astype(jnp.float32).T, wet.astype(jnp.float32), precision=HIGH)
        return carry, None

    coupling, unused = lax.scan(accumulate, jnp.zeros((MS, MA), jnp.float32), jnp.arange(devices, dtype=jnp.int32))

    ds_re, ds_im = modal_terms(shell_freq, shell_loss, freqs)
    da_re, da_im = modal_terms(cavity_freq, cavity_loss, freqs)
    free_re, free_im = divide_complex(jnp.broadcast_to(cavity_source[None, :], da_re.shape), jnp.zeros_like(da_re), da_re, da_im)
    squared = (freqs * freqs)[:, None]
    coupled_re = jnp.zeros_like(free_re)
    coupled_im = jnp.zeros_like(free_im)
    for section in range(SECTIONS):
        amounts = jnp.concatenate([free_re + coupled_re, free_im + coupled_im], 0)
        loads = jnp.dot(amounts, coupling.T, precision=HIGH)
        struct_re, struct_im = divide_complex(modal_force[None, :] + loads[:F], loads[F:], ds_re, ds_im)
        back = jnp.dot(jnp.concatenate([struct_re, struct_im], 0), coupling, precision=HIGH)
        coupled_re, coupled_im = divide_complex(squared * back[:F], squared * back[F:], da_re, da_im)
    modal_structure = jnp.stack([struct_re, struct_im])

    free_amps = lax.optimization_barrier(jnp.concatenate([free_re, free_im], 0).astype(jnp.bfloat16))
    coupled_amps = lax.optimization_barrier(jnp.concatenate([coupled_re, coupled_im], 0).astype(jnp.bfloat16))
    amplitudes = free_amps.astype(jnp.float32) + coupled_amps.astype(jnp.float32)

    def recover(block):
        return jnp.dot(block.astype(jnp.float32), amplitudes.T, precision=HIGH).astype(jnp.bfloat16)

    pressure = lax.map(recover, fluid_blocks).reshape(devices * FD, 2 * F)
    return pressure, modal_structure
```

```python
import functools

import jax
import jax.numpy as jnp
from jax import lax
from jax.experimental import pallas as pl
from jax.experimental.pallas import tpu as pltpu
from jax.sharding import PartitionSpec as P

SECTIONS = 4
MESH = pl.DeviceIdType.MESH
LANES = 128
DIGITS = (("z", 8), ("xh", 2), ("y", 4), ("xl", 2), ("c", 2))
PLANE = ("xh", "y", "xl")
STACK = ("z", "c")


def sizes_of(names):
    table = dict(DIGITS)
    return [table[name] for name in names]


def offsets_of(names):
    places = [()]
    for size in sizes_of(names):
        places = [place + (step,) for place in places for step in range(size)]
    return places[1:]


def own_digits():
    fluid, grp = lax.axis_index("fluid"), lax.axis_index("grp")
    return {
        "z": fluid // 8,
        "xh": (fluid // 4) % 2,
        "y": fluid % 4,
        "xl": grp // 2,
        "c": grp % 2,
    }


def moved(digits, names, offset):
    there = dict(digits)
    for name, size, step in zip(names, sizes_of(names), offset):
        there[name] = lax.rem(digits[name] + step, size)
    return there


def place_of(digits):
    return (digits["z"] * 8 + digits["xh"] * 4 + digits["y"], digits["xl"] * 2 + digits["c"])


def rank_of(digits, names):
    rank = 0
    for name, size in zip(names, sizes_of(names)):
        rank = rank * size + digits[name]
    return rank


def gather_kernel(modes_ref, shell_ref, fluid_ref, node_ref, weight_ref, out_ref, wet_ref, pick_ref):
    step = pl.program_id(0)
    depth = modes_ref.shape[1]
    slots = fluid_ref.shape[1]
    block = 256

    def one_hot(rows, base, picks):
        number = lax.broadcasted_iota(jnp.int32, (rows, picks.shape[1]), 0) + base
        return jnp.where(number == picks, 1.0, 0.0).astype(jnp.bfloat16)

    @pl.when(step == 0)
    def _():
        for first in range(0, slots, block):
            span = pl.ds(first, block)
            hot = one_hot(shell_ref.shape[1], 0, node_ref[:, span])
            pick_ref[:, span] = jnp.dot(
                shell_ref[...], hot, preferred_element_type=jnp.float32
            ).astype(jnp.bfloat16)

    for first in range(0, slots, block):
        span = pl.ds(first, block)
        hot = one_hot(depth, step * depth, fluid_ref[:, span])
        part = jnp.dot(modes_ref[...], hot, preferred_element_type=jnp.float32)

        @pl.when(step == 0)
        def _():
            wet_ref[:, span] = part

        @pl.when(step > 0)
        def _():
            wet_ref[:, span] += part

    @pl.when(step == pl.num_programs(0) - 1)
    def _():
        wet = (wet_ref[...] * weight_ref[...]).astype(jnp.bfloat16)
        total = lax.dot_general(
            wet, pick_ref[...], (((1,), (1,)), ((), ())), preferred_element_type=jnp.float32
        )
        rows = total.shape[0]
        columns = total.shape[1]
        total = jnp.concatenate(
            [total, jnp.zeros((rows, -columns % LANES), jnp.float32)], 1
        ).astype(jnp.bfloat16)
        for part in range(total.shape[1] // LANES):
            out_ref[pl.ds(part * rows, rows), :] = total[:, part * LANES : (part + 1) * LANES]
        used = rows * (total.shape[1] // LANES)
        out_ref[pl.ds(used, out_ref.shape[0] - used), :] = jnp.zeros(
            (out_ref.shape[0] - used, LANES), jnp.bfloat16
        )


def partial_coupling(modes, shell, fluid_nodes, shell_nodes, weights, rows):
    cavity, depth = modes.shape
    slots = fluid_nodes.shape[1]
    chunk = 1024
    whole = lambda shape: pl.BlockSpec(shape, lambda k: (0, 0))
    return pl.pallas_call(
        gather_kernel,
        grid=(depth // chunk,),
        in_specs=[
            pl.BlockSpec((cavity, chunk), lambda k: (0, k)),
            whole(shell.shape),
            whole((1, slots)),
            whole((1, slots)),
            whole((1, slots)),
        ],
        out_specs=whole((rows, LANES)),
        out_shape=jax.ShapeDtypeStruct((rows, LANES), jnp.bfloat16),
        scratch_shapes=[
            pltpu.VMEM((cavity, slots), jnp.float32),
            pltpu.VMEM((shell.shape[0], slots), jnp.bfloat16),
        ],
        compiler_params=pltpu.CompilerParams(
            dimension_semantics=("arbitrary",), vmem_limit_bytes=48 << 20
        ),
    )(modes, shell, fluid_nodes, shell_nodes, weights)


def column_of(row):
    size = row.shape[1]
    below = lax.broadcasted_iota(jnp.int32, (size, size), 0)
    across = lax.broadcasted_iota(jnp.int32, (size, size), 1)
    spread = jnp.where(below == across, jnp.broadcast_to(row, (size, size)), 0.0)
    return jnp.sum(spread, axis=1, keepdims=True)


def inverse_terms(omega, loss, squared):
    stiff = omega * omega
    real_part = stiff - squared
    imag_part = jnp.broadcast_to(loss * stiff, real_part.shape)
    scale = real_part * real_part + imag_part * imag_part
    return real_part / scale, imag_part / scale


def solve_kernel(
    part_ref,
    shell_freq_ref,
    shell_loss_ref,
    cavity_freq_ref,
    cavity_loss_ref,
    freqs_ref,
    force_ref,
    source_ref,
    amps_ref,
    structure_ref,
    plane_ref,
    mine_ref,
    stack_ref,
    full_ref,
    send_sem,
    recv_sem,
):
    digits = own_digits()
    plane, stack = offsets_of(PLANE), offsets_of(STACK)
    size = mine_ref.shape[0]
    barrier = pltpu.get_barrier_semaphore()
    for names, offsets in ((PLANE, plane), (STACK, stack)):
        for offset in offsets:
            pl.semaphore_signal(
                barrier,
                inc=1,
                device_id=place_of(moved(digits, names, offset)),
                device_id_type=MESH,
            )
    pl.semaphore_wait(barrier, len(plane) + len(stack))

    def rows_of(rank):
        return pl.ds(pl.multiple_of(rank * size, size), size)

    for slot, offset in enumerate(plane):
        there = moved(digits, PLANE, offset)
        pltpu.make_async_remote_copy(
            src_ref=part_ref.at[rows_of(rank_of(there, PLANE))],
            dst_ref=plane_ref.at[slot],
            send_sem=send_sem.at[0],
            recv_sem=recv_sem.at[0],
            device_id=place_of(there),
            device_id_type=MESH,
        ).start()

    frequencies = column_of(freqs_ref[...])
    squared = frequencies * frequencies
    shell_p, shell_q = inverse_terms(shell_freq_ref[...], shell_loss_ref[...], squared)
    cavity_p, cavity_q = inverse_terms(cavity_freq_ref[...], cavity_loss_ref[...], squared)
    base_re = source_ref[...] * cavity_p
    base_im = -source_ref[...] * cavity_q
    back_p, back_q = squared * cavity_p, squared * cavity_q

    pltpu.make_async_copy(plane_ref, plane_ref, recv_sem.at[0]).wait()
    own = rank_of(digits, PLANE)
    mine_ref[...] = (
        part_ref[rows_of(own), :].astype(jnp.float32)
        + jnp.sum(plane_ref[...].astype(jnp.float32), axis=0)
    ).astype(jnp.bfloat16)

    for slot, offset in enumerate(stack):
        pltpu.make_async_remote_copy(
            src_ref=mine_ref,
            dst_ref=stack_ref.at[slot],
            send_sem=send_sem.at[1],
            recv_sem=recv_sem.at[1],
            device_id=place_of(moved(digits, STACK, offset)),
            device_id_type=MESH,
        ).start()
    pltpu.make_async_copy(stack_ref, stack_ref, recv_sem.at[1]).wait()
    full_ref[rows_of(own), :] = (
        mine_ref[...].astype(jnp.float32)
        + jnp.sum(stack_ref[...].astype(jnp.float32), axis=0)
    ).astype(jnp.bfloat16)

    for offset in plane:
        pltpu.make_async_remote_copy(
            src_ref=full_ref.at[rows_of(own)],
            dst_ref=full_ref.at[rows_of(own)],
            send_sem=send_sem.at[2],
            recv_sem=recv_sem.at[2],
            device_id=place_of(moved(digits, PLANE, offset)),
            device_id_type=MESH,
        ).start()
    pltpu.make_async_copy(plane_ref, plane_ref, recv_sem.at[2]).wait()

    cavity = base_re.shape[1]
    shells = shell_p.shape[1]
    count = squared.shape[0]
    coupling = jnp.concatenate(
        [full_ref[pl.ds(at * cavity, cavity), :] for at in range(pl.cdiv(shells, LANES))], 1
    )[:, :shells]
    force = force_ref[...]
    real, imag = base_re, base_im
    for section in range(SECTIONS):
        loads = jnp.dot(
            jnp.concatenate([real, imag], 0).astype(jnp.bfloat16),
            coupling,
            preferred_element_type=jnp.float32,
        )
        load_re, load_im = force + loads[:count], loads[count:]
        struct_re = load_re * shell_p + load_im * shell_q
        struct_im = load_im * shell_p - load_re * shell_q
        back = lax.dot_general(
            jnp.concatenate([struct_re, struct_im], 0).astype(jnp.bfloat16),
            coupling,
            (((1,), (1,)), ((), ())),
            preferred_element_type=jnp.float32,
        )
        back_re, back_im = back[:count], back[count:]
        real = base_re + (back_re * back_p + back_im * back_q)
        imag = base_im + (back_im * back_p - back_re * back_q)
    amps_ref[...] = jnp.concatenate([real, imag], 0).astype(jnp.bfloat16)
    structure_ref[0] = struct_re
    structure_ref[1] = struct_im

    pltpu.make_async_copy(plane_ref, plane_ref, send_sem.at[0]).wait()
    pltpu.make_async_copy(stack_ref, stack_ref, send_sem.at[1]).wait()
    pltpu.make_async_copy(plane_ref, plane_ref, send_sem.at[2]).wait()


def solve(part, terms, count, shells, cavity):
    planes, stacks = len(offsets_of(PLANE)), len(offsets_of(STACK))
    size = part.shape[0] // (planes + 1)
    inside = pl.BlockSpec(memory_space=pltpu.VMEM)
    return pl.pallas_call(
        solve_kernel,
        in_specs=[inside] * (1 + len(terms)),
        out_specs=[inside] * 2,
        out_shape=[
            jax.ShapeDtypeStruct((2 * count, cavity), jnp.bfloat16),
            jax.ShapeDtypeStruct((2, count, shells), jnp.float32),
        ],
        scratch_shapes=[
            pltpu.VMEM((planes, size, LANES), jnp.bfloat16),
            pltpu.VMEM((size, LANES), jnp.bfloat16),
            pltpu.VMEM((stacks, size, LANES), jnp.bfloat16),
            pltpu.VMEM(part.shape, jnp.bfloat16),
            pltpu.SemaphoreType.DMA((3,)),
            pltpu.SemaphoreType.DMA((3,)),
        ],
        compiler_params=pltpu.CompilerParams(
            collective_id=0, has_side_effects=True, vmem_limit_bytes=32 << 20
        ),
    )(part, *terms)


def field_kernel(amps_ref, modes_ref, structure_ref, pressure_ref, own_ref):
    field = jnp.dot(amps_ref[...], modes_ref[...], preferred_element_type=jnp.float32)
    pressure_ref[...] = field.T.astype(jnp.bfloat16)

    @pl.when(pl.program_id(0) == 0)
    def _():
        count = own_ref.shape[1]
        first = pl.multiple_of(lax.axis_index("grp") * count, count)
        own_ref[...] = structure_ref[:, pl.ds(first, count), :]


def field(amps, modes, structure, groups):
    cavity, depth = modes.shape
    chunk = 1024
    parts, count, shells = structure.shape
    own = (parts, count // groups, shells)
    return pl.pallas_call(
        field_kernel,
        grid=(depth // chunk,),
        in_specs=[
            pl.BlockSpec(amps.shape, lambda k: (0, 0)),
            pl.BlockSpec((cavity, chunk), lambda k: (0, k)),
            pl.BlockSpec(structure.shape, lambda k: (0, 0, 0)),
        ],
        out_specs=[
            pl.BlockSpec((chunk, amps.shape[0]), lambda k: (k, 0)),
            pl.BlockSpec(own, lambda k: (0, 0, 0)),
        ],
        out_shape=[
            jax.ShapeDtypeStruct((depth, amps.shape[0]), jnp.bfloat16),
            jax.ShapeDtypeStruct(own, jnp.float32),
        ],
        compiler_params=pltpu.CompilerParams(dimension_semantics=("arbitrary",)),
    )(amps, modes, structure)


def on_device(
    acoustic_modes,
    shell_modes,
    wet_counts,
    fluid_nodes,
    shell_nodes,
    wet_area,
    shell_freq,
    shell_loss,
    cavity_freq,
    cavity_loss,
    freqs,
    modal_force,
    cavity_source,
):
    groups = lax.axis_size("grp")
    slots = fluid_nodes.shape[0]
    live = jnp.arange(slots, dtype=jnp.int32) < wet_counts[0]
    weights = jnp.where(live, wet_area, 0.0)
    modes = acoustic_modes.T
    shells, cavity = shell_modes.shape[1], acoustic_modes.shape[1]
    unit = 16 * (len(offsets_of(PLANE)) + 1)
    rows = pl.cdiv(cavity * pl.cdiv(shells, LANES), unit) * unit
    part = partial_coupling(
        modes,
        shell_modes.T,
        fluid_nodes[None, :],
        shell_nodes[None, :],
        weights[None, :],
        rows,
    )
    terms = (shell_freq, shell_loss, cavity_freq, cavity_loss, freqs, modal_force, cavity_source)
    amps, structure = solve(
        part, [term[None, :] for term in terms], freqs.shape[0], shells, cavity
    )
    return tuple(field(amps, modes, structure, groups))


def solution(mesh):
    both = P(("fluid", "grp"))
    placed = (P(("fluid", "grp"), None), P("fluid", None)) + (both,) * 4 + (P(),) * 7
    return jax.shard_map(
        on_device,
        mesh=mesh,
        in_specs=placed,
        out_specs=(P(("fluid", "grp"), None), P(None, "grp", None)),
        check_vma=False,
    )
```

```python
import jax
import jax.numpy as jnp
from jax import lax
from jax.experimental import pallas as pl
from jax.experimental.pallas import tpu as pltpu
from jax.sharding import PartitionSpec as P

SECTIONS = 4
MESH = pl.DeviceIdType.MESH
LANES = 128
SIZES = {"z": 8, "xh": 2, "y": 4, "xl": 2, "c": 2}
PLANE = ("xh", "y", "xl", "c")
STACK = ("z",)
CHUNKS = 8
TAIL = 4


def offsets_of(names):
    places = [()]
    for name in names:
        places = [place + (step,) for place in places for step in range(SIZES[name])]
    return places[1:]


def own_digits():
    fluid, grp = lax.axis_index("fluid"), lax.axis_index("grp")
    return {
        "z": fluid // 8,
        "xh": (fluid // 4) % 2,
        "y": fluid % 4,
        "xl": grp // 2,
        "c": grp % 2,
    }


def moved(digits, names, offset):
    there = dict(digits)
    for name, step in zip(names, offset):
        if step:
            there[name] = lax.rem(digits[name] + step, SIZES[name])
    return there


def place_of(digits):
    return (digits["z"] * 8 + digits["xh"] * 4 + digits["y"], digits["xl"] * 2 + digits["c"])


def rank_of(digits, names):
    rank = 0
    for name in names:
        rank = rank * SIZES[name] + digits[name]
    return rank


def column_of(row):
    size = row.shape[1]
    below = lax.broadcasted_iota(jnp.int32, (size, size), 0)
    across = lax.broadcasted_iota(jnp.int32, (size, size), 1)
    spread = jnp.where(below == across, jnp.broadcast_to(row, (size, size)), 0.0)
    return jnp.sum(spread, axis=1, keepdims=True)


def inverse_terms(omega, loss, squared):
    stiff = omega * omega
    real_part = stiff - squared
    imag_part = jnp.broadcast_to(loss * stiff, real_part.shape)
    scale = real_part * real_part + imag_part * imag_part
    return real_part / scale, imag_part / scale


def pad_lanes(values, width):
    if values.shape[1] == width:
        return values
    rest = jnp.zeros((values.shape[0], width - values.shape[1]), values.dtype)
    return jnp.concatenate([values, rest], 1)


def pad_rows(values, height):
    if values.shape[0] == height:
        return values
    rest = jnp.zeros((height - values.shape[0], values.shape[1]), values.dtype)
    return jnp.concatenate([values, rest], 0)


def tail_height(shells):
    return pl.cdiv(pl.cdiv(shells, TAIL), 16) * 16


def rows_needed(shells, cavity, parts):
    high = pl.cdiv(shells, 16) * 16
    used = high * (cavity // LANES) + tail_height(shells)
    return pl.cdiv(used, 16 * parts) * 16 * parts


def pack(total, out_ref):
    shells, cavity = total.shape
    high = pl.cdiv(shells, 16) * 16
    full = cavity // LANES
    for at in range(full):
        piece = pad_rows(total[:, at * LANES : (at + 1) * LANES], high)
        out_ref[pl.ds(at * high, high), :] = piece.astype(out_ref.dtype)
    tall, wide = tail_height(shells), LANES // TAIL
    rest = pad_lanes(pad_rows(total[:, full * LANES :], tall * TAIL), wide)
    tail = jnp.concatenate([rest[at * tall : (at + 1) * tall] for at in range(TAIL)], 1)
    height = out_ref.shape[0] - full * high
    out_ref[pl.ds(full * high, height), :] = pad_rows(tail, height).astype(out_ref.dtype)


def unpack(full_ref, shells, cavity):
    high = pl.cdiv(shells, 16) * 16
    full = cavity // LANES
    tall, wide = tail_height(shells), LANES // TAIL
    blocks = [full_ref[pl.ds(at * high, high), :] for at in range(full)]
    tail = full_ref[pl.ds(full * high, tall), :].astype(jnp.float32)
    rest = [tail[:, at * wide : at * wide + cavity - full * LANES] for at in range(TAIL)]
    rest = jnp.concatenate(rest, 0)[:high].astype(full_ref.dtype)
    return jnp.concatenate(blocks + [rest], 1)[:shells]


def outer(value):
    return pltpu.with_memory_space_constraint(value, pltpu.HBM)


def gather_kernel(
    modes_hbm,
    shell_hbm,
    count_ref,
    fluid_hbm,
    node_hbm,
    area_hbm,
    part_ref,
    modes_ref,
    shell_ref,
    fluid_ref,
    node_ref,
    area_ref,
    table_ref,
    rows_ref,
    pick_ref,
    area_rows_ref,
    modes_sem,
    small_sem,
):
    cavity, depth = modes_ref.shape
    shells, shell_depth = shell_ref.shape
    slots = fluid_ref.shape[0]
    chunk, span = depth // CHUNKS, slots // CHUNKS
    lane_blocks = pl.cdiv(cavity, LANES)

    pairs = [
        (shell_hbm, shell_ref),
        (node_hbm, node_ref),
        (area_hbm, area_ref),
        (fluid_hbm, fluid_ref),
    ]
    small = [
        pltpu.make_async_copy(source, target, small_sem.at[at])
        for at, (source, target) in enumerate(pairs)
    ]
    large = [
        pltpu.make_async_copy(
            modes_hbm.at[:, pl.ds(at * chunk, chunk)],
            modes_ref.at[:, pl.ds(at * chunk, chunk)],
            modes_sem.at[at],
        )
        for at in range(CHUNKS)
    ]
    for copy in small + large:
        copy.start()
    for copy in small:
        copy.wait()
    count = count_ref[0]
    for at in range(CHUNKS):
        here = pl.ds(at * span, span)
        slot = lax.broadcasted_iota(jnp.int32, (1, span), 1) + at * span
        node = jnp.where(slot < count, node_ref[here].reshape(1, span), -1)
        number = lax.broadcasted_iota(jnp.int32, (shell_depth, span), 0)
        hot = jnp.where(number == node, 1.0, 0.0).astype(jnp.bfloat16)
        pick_ref[:, here] = jnp.dot(
            shell_ref[...], hot, preferred_element_type=jnp.float32
        ).astype(jnp.bfloat16)
        area = area_ref[here].reshape(1, span)
        area_rows_ref[here, :] = jnp.broadcast_to(area, (LANES, span)).T
        large[at].wait()
        for block in range(lane_blocks):
            first = block * LANES
            wide = min(LANES, cavity - first)
            piece = modes_ref[first : first + wide, at * chunk : (at + 1) * chunk].T
            table_ref[pl.ds(at * chunk * lane_blocks + block, chunk, stride=lane_blocks), :] = (
                pad_lanes(piece.astype(jnp.float32), LANES)
            )

    unroll = 16

    def gather(step, carry):
        for at in range(unroll):
            slot = step * unroll + at
            first = pl.multiple_of(fluid_ref[slot] * lane_blocks, lane_blocks)
            rows_ref[pl.ds(pl.multiple_of(slot * lane_blocks, lane_blocks), lane_blocks), :] = (
                table_ref[pl.ds(first, lane_blocks), :]
            )
        return carry

    lax.fori_loop(0, slots // unroll, gather, 0)
    area = area_rows_ref[...]
    wet = jnp.concatenate(
        [
            (rows_ref[pl.ds(block, slots, stride=lane_blocks), :] * area).astype(jnp.bfloat16)
            for block in range(lane_blocks)
        ],
        1,
    )
    total = jnp.dot(pick_ref[...], wet, preferred_element_type=jnp.float32)
    pack(total[:, :cavity], part_ref)


def partial_coupling(modes, shell, count, fluid_nodes, shell_nodes, area):
    cavity, depth = modes.shape
    shells = shell.shape[0]
    slots = fluid_nodes.shape[0]
    rows = rows_needed(shells, cavity, len(offsets_of(PLANE)) + 1)
    lane_blocks = pl.cdiv(cavity, LANES)
    outside = pl.BlockSpec(memory_space=pltpu.HBM)
    inside = pl.BlockSpec(memory_space=pltpu.VMEM)
    return pl.pallas_call(
        gather_kernel,
        in_specs=[outside] * 2 + [pl.BlockSpec(memory_space=pltpu.SMEM)] + [outside] * 3,
        out_specs=[inside] * 2,
        out_shape=[
            jax.ShapeDtypeStruct((rows, LANES), jnp.bfloat16),
            jax.ShapeDtypeStruct(modes.shape, modes.dtype),
        ],
        scratch_shapes=[
            pltpu.VMEM(shell.shape, shell.dtype),
            pltpu.SMEM((slots,), jnp.int32),
            pltpu.VMEM((slots,), jnp.int32),
            pltpu.VMEM((slots,), jnp.float32),
            pltpu.VMEM((depth * lane_blocks, LANES), jnp.float32),
            pltpu.VMEM((slots * lane_blocks, LANES), jnp.float32),
            pltpu.VMEM((shells, slots), jnp.bfloat16),
            pltpu.VMEM((slots, LANES), jnp.float32),
            pltpu.SemaphoreType.DMA((CHUNKS,)),
            pltpu.SemaphoreType.DMA((len((shell, fluid_nodes, shell_nodes, area)),)),
        ],
        compiler_params=pltpu.CompilerParams(vmem_limit_bytes=44 << 20),
    )(outer(modes), outer(shell), count, outer(fluid_nodes), outer(shell_nodes), outer(area))


def solve_kernel(part_ref, *rest):
    terms_hbm = rest[:7]
    amps_ref, structure_ref = rest[7:9]
    terms = rest[9:16]
    plane_ref, mine_ref, stack_ref, full_ref, term_sem, send_sem, recv_sem = rest[16:]

    digits = own_digits()
    plane, stack = offsets_of(PLANE), offsets_of(STACK)
    barrier = pltpu.get_barrier_semaphore()
    for names, offsets in ((PLANE, plane), (STACK, stack)):
        for offset in offsets:
            pl.semaphore_signal(
                barrier,
                inc=1,
                device_id=place_of(moved(digits, names, offset)),
                device_id_type=MESH,
            )
    small = [
        pltpu.make_async_copy(source, target, term_sem.at[at])
        for at, (source, target) in enumerate(zip(terms_hbm, terms))
    ]
    for copy in small:
        copy.start()

    size = mine_ref.shape[0]
    own = rank_of(digits, PLANE)

    def rows_of(rank):
        return pl.ds(pl.multiple_of(rank * size, size), size)

    pl.semaphore_wait(barrier, len(plane) + len(stack))
    for slot, offset in enumerate(plane):
        there = moved(digits, PLANE, offset)
        pltpu.make_async_remote_copy(
            src_ref=part_ref.at[rows_of(rank_of(there, PLANE))],
            dst_ref=plane_ref.at[slot],
            send_sem=send_sem.at[0],
            recv_sem=recv_sem.at[0],
            device_id=place_of(there),
            device_id_type=MESH,
        ).start()

    for copy in small:
        copy.wait()
    shells, cavity = terms[0].shape[0], terms[2].shape[0]
    shell_freq, shell_loss, cavity_freq, cavity_loss, freqs, force, source = [
        term[...].reshape(1, term.shape[0]) for term in terms
    ]
    frequencies = column_of(freqs)
    squared = frequencies * frequencies
    shell_p, shell_q = inverse_terms(shell_freq, shell_loss, squared)
    cavity_p, cavity_q = inverse_terms(cavity_freq, cavity_loss, squared)
    base_re = source * cavity_p
    base_im = -source * cavity_q
    back_p, back_q = squared * cavity_p, squared * cavity_q

    pltpu.make_async_copy(plane_ref, plane_ref, recv_sem.at[0]).wait()
    mine_ref[...] = (
        part_ref[rows_of(own), :].astype(jnp.float32)
        + jnp.sum(plane_ref[...].astype(jnp.float32), axis=0)
    ).astype(jnp.bfloat16)

    for slot, offset in enumerate(stack):
        pltpu.make_async_remote_copy(
            src_ref=mine_ref,
            dst_ref=stack_ref.at[slot],
            send_sem=send_sem.at[1],
            recv_sem=recv_sem.at[1],
            device_id=place_of(moved(digits, STACK, offset)),
            device_id_type=MESH,
        ).start()
    pltpu.make_async_copy(stack_ref, stack_ref, recv_sem.at[1]).wait()
    full_ref[rows_of(own), :] = (
        mine_ref[...].astype(jnp.float32)
        + jnp.sum(stack_ref[...].astype(jnp.float32), axis=0)
    ).astype(jnp.bfloat16)

    for offset in plane:
        pltpu.make_async_remote_copy(
            src_ref=full_ref.at[rows_of(own)],
            dst_ref=full_ref.at[rows_of(own)],
            send_sem=send_sem.at[2],
            recv_sem=recv_sem.at[2],
            device_id=place_of(moved(digits, PLANE, offset)),
            device_id_type=MESH,
        ).start()
    pltpu.make_async_copy(plane_ref, plane_ref, recv_sem.at[2]).wait()

    coupling = unpack(full_ref, shells, cavity)
    total_freqs = squared.shape[0]
    real, imag = base_re, base_im
    for section in range(SECTIONS):
        loads = lax.dot_general(
            jnp.concatenate([real, imag], 0).astype(jnp.bfloat16),
            coupling,
            (((1,), (1,)), ((), ())),
            preferred_element_type=jnp.float32,
        )
        load_re, load_im = force + loads[:total_freqs], loads[total_freqs:]
        struct_re = load_re * shell_p + load_im * shell_q
        struct_im = load_im * shell_p - load_re * shell_q
        back = jnp.dot(
            jnp.concatenate([struct_re, struct_im], 0).astype(jnp.bfloat16),
            coupling,
            preferred_element_type=jnp.float32,
        )
        back_re, back_im = back[:total_freqs], back[total_freqs:]
        coupled_re = back_re * back_p + back_im * back_q
        coupled_im = back_im * back_p - back_re * back_q
        real, imag = base_re + coupled_re, base_im + coupled_im
    for at, values in enumerate((base_re, base_im, coupled_re, coupled_im)):
        amps_ref[pl.ds(at * total_freqs, total_freqs), :] = values.astype(jnp.bfloat16)
    structure_ref[0] = struct_re
    structure_ref[1] = struct_im

    pltpu.make_async_copy(plane_ref, plane_ref, send_sem.at[0]).wait()
    pltpu.make_async_copy(stack_ref, stack_ref, send_sem.at[1]).wait()
    pltpu.make_async_copy(plane_ref, plane_ref, send_sem.at[2]).wait()


def solve(part, terms):
    shells, cavity, total_freqs = terms[0].shape[0], terms[2].shape[0], terms[4].shape[0]
    planes, stacks = len(offsets_of(PLANE)), len(offsets_of(STACK))
    size = part.shape[0] // (planes + 1)
    outside = pl.BlockSpec(memory_space=pltpu.HBM)
    inside = pl.BlockSpec(memory_space=pltpu.VMEM)
    return pl.pallas_call(
        solve_kernel,
        in_specs=[inside] + [outside] * len(terms),
        out_specs=[inside] * 2,
        out_shape=[
            jax.ShapeDtypeStruct((4 * total_freqs, cavity), jnp.bfloat16),
            jax.ShapeDtypeStruct((2, total_freqs, shells), jnp.float32),
        ],
        scratch_shapes=[pltpu.VMEM(term.shape, term.dtype) for term in terms]
        + [
            pltpu.VMEM((planes, size, LANES), jnp.bfloat16),
            pltpu.VMEM((size, LANES), jnp.bfloat16),
            pltpu.VMEM((stacks, size, LANES), jnp.bfloat16),
            pltpu.VMEM(part.shape, jnp.bfloat16),
            pltpu.SemaphoreType.DMA((len(terms),)),
            pltpu.SemaphoreType.DMA((3,)),
            pltpu.SemaphoreType.DMA((3,)),
        ],
        compiler_params=pltpu.CompilerParams(
            collective_id=0, has_side_effects=True, vmem_limit_bytes=24 << 20
        ),
    )(part, *[outer(term) for term in terms])


def field_kernel(amps_ref, modes_ref, structure_ref, pressure_hbm, own_ref, held_ref, out_sem):
    chunk = held_ref.shape[1]
    half = held_ref.shape[2]
    copies = []
    for at in range(held_ref.shape[0]):
        both = jnp.dot(
            amps_ref[...],
            modes_ref[:, at * chunk : (at + 1) * chunk],
            preferred_element_type=jnp.float32,
        )
        held_ref[at] = (both[:half] + both[half:]).T.astype(jnp.bfloat16)
        copies.append(
            pltpu.make_async_copy(
                held_ref.at[at], pressure_hbm.at[pl.ds(at * chunk, chunk)], out_sem.at[at]
            )
        )
        copies[-1].start()
    count = own_ref.shape[1]
    first = pl.multiple_of(lax.axis_index("grp") * count, count)
    own_ref[...] = structure_ref[:, pl.ds(first, count), :]
    for copy in copies:
        copy.wait()


def field(amps, modes, structure, groups):
    depth = modes.shape[1]
    parts, count, shells = structure.shape
    half = amps.shape[0] // 2
    inside = pl.BlockSpec(memory_space=pltpu.VMEM)
    return pl.pallas_call(
        field_kernel,
        in_specs=[inside] * 3,
        out_specs=[pl.BlockSpec(memory_space=pltpu.HBM), inside],
        out_shape=[
            jax.ShapeDtypeStruct((depth, half), jnp.bfloat16),
            jax.ShapeDtypeStruct((parts, count // groups, shells), jnp.float32),
        ],
        scratch_shapes=[
            pltpu.VMEM((CHUNKS, depth // CHUNKS, half), jnp.bfloat16),
            pltpu.SemaphoreType.DMA((CHUNKS,)),
        ],
        compiler_params=pltpu.CompilerParams(vmem_limit_bytes=24 << 20),
    )(amps, modes, structure)


def on_device(acoustic_modes, shell_modes, wet_counts, fluid_nodes, shell_nodes, wet_area, *terms):
    part, modes = partial_coupling(
        acoustic_modes.T, shell_modes.T, wet_counts, fluid_nodes, shell_nodes, wet_area
    )
    amps, structure = solve(part, terms)
    return tuple(field(amps, modes, structure, lax.axis_size("grp")))


def solution(mesh):
    both = P(("fluid", "grp"))
    placed = (P(("fluid", "grp"), None), P("fluid", None)) + (both,) * 4 + (P(),) * 7
    return jax.shard_map(
        on_device,
        mesh=mesh,
        in_specs=placed,
        out_specs=(P(("fluid", "grp"), None), P(None, "grp", None)),
        check_vma=False,
    )
```

```python
import jax
import jax.numpy as jnp
from jax import lax
from jax.experimental import pallas as pl
from jax.experimental.pallas import tpu as pltpu
from jax.sharding import PartitionSpec as P

SECTIONS = 4
MESH = pl.DeviceIdType.MESH
LANES = 128
SIZES = {"z": 8, "xh": 2, "y": 4, "xl": 2, "c": 2}
PLANE = ("xh", "y", "xl", "c")
STACK = ("z",)
CHUNKS = 8
TAIL = 4


def offsets_of(names):
    places = [()]
    for name in names:
        places = [place + (step,) for place in places for step in range(SIZES[name])]
    return sorted(places[1:], key=lambda place: -hops(names, place))


def hops(names, place):
    return sum(
        min(step, SIZES[name] - step) for name, step in zip(names, place) if name != "c"
    )


def own_digits():
    fluid, grp = lax.axis_index("fluid"), lax.axis_index("grp")
    digits = {
        "z": fluid // 8,
        "xh": (fluid // 4) % 2,
        "y": fluid % 4,
        "xl": grp // 2,
        "c": grp % 2,
    }
    for name, size in SIZES.items():
        for step in range(1, size):
            digits[name, step] = lax.rem(digits[name] + step, size)
    return digits


def moved(digits, names, offset):
    there = dict(digits)
    for name, step in zip(names, offset):
        if step:
            there[name] = digits[name, step]
    return there


def place_of(digits):
    return (digits["z"] * 8 + digits["xh"] * 4 + digits["y"], digits["xl"] * 2 + digits["c"])


def rank_of(digits, names):
    rank = 0
    for name in names:
        rank = rank * SIZES[name] + digits[name]
    return rank


def column_of(row):
    size = row.shape[1]
    below = lax.broadcasted_iota(jnp.int32, (size, size), 0)
    across = lax.broadcasted_iota(jnp.int32, (size, size), 1)
    spread = jnp.where(below == across, jnp.broadcast_to(row, (size, size)), 0.0)
    return jnp.sum(spread, axis=1, keepdims=True)


def inverse_terms(omega, loss, squared):
    stiff = omega * omega
    real_part = stiff - squared
    imag_part = jnp.broadcast_to(loss * stiff, real_part.shape)
    scale = real_part * real_part + imag_part * imag_part
    return real_part / scale, imag_part / scale


def pad_lanes(values, width):
    if values.shape[1] == width:
        return values
    rest = jnp.zeros((values.shape[0], width - values.shape[1]), values.dtype)
    return jnp.concatenate([values, rest], 1)


def pad_rows(values, height):
    if values.shape[0] == height:
        return values
    rest = jnp.zeros((height - values.shape[0], values.shape[1]), values.dtype)
    return jnp.concatenate([values, rest], 0)


def tail_height(shells):
    return pl.cdiv(pl.cdiv(shells, TAIL), 16) * 16


def rows_needed(shells, cavity, parts):
    high = pl.cdiv(shells, 16) * 16
    used = high * (cavity // LANES) + tail_height(shells)
    return pl.cdiv(used, 16 * parts) * 16 * parts


def pack(total, out_ref):
    shells, cavity = total.shape
    high = pl.cdiv(shells, 16) * 16
    full = cavity // LANES
    for at in range(full):
        piece = pad_rows(total[:, at * LANES : (at + 1) * LANES], high)
        out_ref[pl.ds(at * high, high), :] = piece.astype(out_ref.dtype)
    tall, wide = tail_height(shells), LANES // TAIL
    rest = pad_lanes(pad_rows(total[:, full * LANES :], tall * TAIL), wide)
    tail = jnp.concatenate([rest[at * tall : (at + 1) * tall] for at in range(TAIL)], 1)
    height = out_ref.shape[0] - full * high
    out_ref[pl.ds(full * high, height), :] = pad_rows(tail, height).astype(out_ref.dtype)


def unpack(full_ref, shells, cavity):
    high = pl.cdiv(shells, 16) * 16
    full = cavity // LANES
    tall, wide = tail_height(shells), LANES // TAIL
    blocks = [full_ref[pl.ds(at * high, high), :] for at in range(full)]
    tail = full_ref[pl.ds(full * high, tall), :].astype(jnp.float32)
    rest = [tail[:, at * wide : at * wide + cavity - full * LANES] for at in range(TAIL)]
    rest = jnp.concatenate(rest, 0)[:high].astype(full_ref.dtype)
    return jnp.concatenate(blocks + [rest], 1)[:shells]


def outer(value):
    return pltpu.with_memory_space_constraint(value, pltpu.HBM)


def main_kernel(
    modes_hbm,
    shell_hbm,
    count_ref,
    fluid_hbm,
    node_hbm,
    area_hbm,
    *rest,
):
    terms_hbm = rest[:7]
    amps_ref, structure_ref, modes_ref = rest[7:10]
    shell_ref, fluid_ref, node_ref, area_ref = rest[10:14]
    terms = rest[14:21]
    table_ref, rows_ref, pick_ref, area_rows_ref = rest[21:25]
    part_ref, plane_ref, mine_ref, stack_ref, full_ref = rest[25:30]
    modes_sem, small_sem, send_sem, recv_sem = rest[30:]

    cavity, depth = modes_ref.shape
    shells, shell_depth = shell_ref.shape
    slots = fluid_ref.shape[0]
    chunk, span = depth // CHUNKS, slots // CHUNKS
    lane_blocks = pl.cdiv(cavity, LANES)

    small = [
        pltpu.make_async_copy(source, target, small_sem.at[at])
        for at, (source, target) in enumerate(
            [
                (shell_hbm, shell_ref),
                (node_hbm, node_ref),
                (area_hbm, area_ref),
                (fluid_hbm, fluid_ref),
            ]
            + list(zip(terms_hbm, terms))
        )
    ]
    large = [
        pltpu.make_async_copy(
            modes_hbm.at[:, pl.ds(at * chunk, chunk)],
            modes_ref.at[:, pl.ds(at * chunk, chunk)],
            modes_sem.at[at],
        )
        for at in range(CHUNKS)
    ]
    small[0].start()
    large[0].start()
    for copy in small[1:] + large[1:]:
        copy.start()

    digits = own_digits()
    plane, stack = offsets_of(PLANE), offsets_of(STACK)
    barrier = pltpu.get_barrier_semaphore()
    for names, offsets in ((PLANE, plane), (STACK, stack)):
        for offset in offsets:
            pl.semaphore_signal(
                barrier,
                inc=1,
                device_id=place_of(moved(digits, names, offset)),
                device_id_type=MESH,
            )

    for copy in small:
        copy.wait()
    count = count_ref[0]
    for at in range(CHUNKS):
        here = pl.ds(at * span, span)
        slot = lax.broadcasted_iota(jnp.int32, (1, span), 1) + at * span
        node = jnp.where(slot < count, node_ref[here].reshape(1, span), -1)
        number = lax.broadcasted_iota(jnp.int32, (shell_depth, span), 0)
        hot = jnp.where(number == node, 1.0, 0.0).astype(jnp.bfloat16)
        pick_ref[:, here] = jnp.dot(
            shell_ref[...], hot, preferred_element_type=jnp.float32
        ).astype(jnp.bfloat16)
        area = area_ref[here].reshape(1, span)
        area_rows_ref[here, :] = jnp.broadcast_to(area, (LANES, span)).T
        large[at].wait()
        for block in range(lane_blocks):
            first = block * LANES
            wide = min(LANES, cavity - first)
            piece = modes_ref[first : first + wide, at * chunk : (at + 1) * chunk].T
            table_ref[pl.ds(at * chunk * lane_blocks + block, chunk, stride=lane_blocks), :] = (
                pad_lanes(piece.astype(jnp.float32), LANES)
            )

    unroll = 16
    pairs_ref = table_ref.reshape(depth // 2, 2 * lane_blocks, LANES)

    def gather(step, carry):
        for at in range(unroll):
            slot = step * unroll + at
            node = fluid_ref[slot]
            pair = pairs_ref[lax.shift_right_logical(node, 1)]
            rows_ref[pl.ds(pl.multiple_of(slot * lane_blocks, lane_blocks), lane_blocks), :] = (
                jnp.where(
                    jnp.bitwise_and(node, 1) == 1, pair[lane_blocks:], pair[:lane_blocks]
                )
            )
        return carry

    lax.fori_loop(0, slots // unroll, gather, 0)
    area = area_rows_ref[...]
    wet = jnp.concatenate(
        [
            (rows_ref[pl.ds(block, slots, stride=lane_blocks), :] * area).astype(jnp.bfloat16)
            for block in range(lane_blocks)
        ],
        1,
    )
    total = jnp.dot(pick_ref[...], wet, preferred_element_type=jnp.float32)
    pack(total[:, :cavity], part_ref)

    size = mine_ref.shape[0]
    own = rank_of(digits, PLANE)

    def rows_of(rank):
        return pl.ds(pl.multiple_of(rank * size, size), size)

    pl.semaphore_wait(barrier, len(plane) + len(stack))
    for slot, offset in enumerate(plane):
        there = moved(digits, PLANE, offset)
        pltpu.make_async_remote_copy(
            src_ref=part_ref.at[rows_of(rank_of(there, PLANE))],
            dst_ref=plane_ref.at[slot],
            send_sem=send_sem.at[0],
            recv_sem=recv_sem.at[0],
            device_id=place_of(there),
            device_id_type=MESH,
        ).start()

    shell_freq, shell_loss, cavity_freq, cavity_loss, freqs, force, source = [
        term[...].reshape(1, term.shape[0]) for term in terms
    ]
    frequencies = column_of(freqs)
    squared = frequencies * frequencies
    shell_p, shell_q = inverse_terms(shell_freq, shell_loss, squared)
    cavity_p, cavity_q = inverse_terms(cavity_freq, cavity_loss, squared)
    base_re = source * cavity_p
    base_im = -source * cavity_q
    back_p, back_q = squared * cavity_p, squared * cavity_q

    pltpu.make_async_copy(plane_ref, plane_ref, recv_sem.at[0]).wait()
    mine_ref[...] = (
        part_ref[rows_of(own), :].astype(jnp.float32)
        + jnp.sum(plane_ref[...].astype(jnp.float32), axis=0)
    ).astype(jnp.bfloat16)

    for slot, offset in enumerate(stack):
        pltpu.make_async_remote_copy(
            src_ref=mine_ref,
            dst_ref=stack_ref.at[slot],
            send_sem=send_sem.at[1],
            recv_sem=recv_sem.at[1],
            device_id=place_of(moved(digits, STACK, offset)),
            device_id_type=MESH,
        ).start()
    pltpu.make_async_copy(stack_ref, stack_ref, recv_sem.at[1]).wait()
    full_ref[rows_of(own), :] = (
        mine_ref[...].astype(jnp.float32)
        + jnp.sum(stack_ref[...].astype(jnp.float32), axis=0)
    ).astype(jnp.bfloat16)

    for offset in plane:
        pltpu.make_async_remote_copy(
            src_ref=full_ref.at[rows_of(own)],
            dst_ref=full_ref.at[rows_of(own)],
            send_sem=send_sem.at[2],
            recv_sem=recv_sem.at[2],
            device_id=place_of(moved(digits, PLANE, offset)),
            device_id_type=MESH,
        ).start()
    pltpu.make_async_copy(plane_ref, plane_ref, recv_sem.at[2]).wait()

    coupling = unpack(full_ref, shells, cavity)
    total_freqs = squared.shape[0]
    real, imag = base_re, base_im
    for section in range(SECTIONS):
        loads = lax.dot_general(
            jnp.concatenate([real, imag], 0).astype(jnp.bfloat16),
            coupling,
            (((1,), (1,)), ((), ())),
            preferred_element_type=jnp.float32,
        )
        load_re, load_im = force + loads[:total_freqs], loads[total_freqs:]
        struct_re = load_re * shell_p + load_im * shell_q
        struct_im = load_im * shell_p - load_re * shell_q
        back = jnp.dot(
            jnp.concatenate([struct_re, struct_im], 0).astype(jnp.bfloat16),
            coupling,
            preferred_element_type=jnp.float32,
        )
        back_re, back_im = back[:total_freqs], back[total_freqs:]
        coupled_re = back_re * back_p + back_im * back_q
        coupled_im = back_im * back_p - back_re * back_q
        real, imag = base_re + coupled_re, base_im + coupled_im
    for at, values in enumerate((base_re, base_im, coupled_re, coupled_im)):
        amps_ref[pl.ds(at * total_freqs, total_freqs), :] = values.astype(jnp.bfloat16)
    structure_ref[0] = struct_re
    structure_ref[1] = struct_im

    pltpu.make_async_copy(plane_ref, plane_ref, send_sem.at[0]).wait()
    pltpu.make_async_copy(stack_ref, stack_ref, send_sem.at[1]).wait()
    pltpu.make_async_copy(plane_ref, plane_ref, send_sem.at[2]).wait()


def amplitudes(modes, shell, count, fluid_nodes, shell_nodes, area, terms, total_freqs):
    cavity, depth = modes.shape
    shells = shell.shape[0]
    slots = fluid_nodes.shape[0]
    planes, stacks = len(offsets_of(PLANE)), len(offsets_of(STACK))
    rows = rows_needed(shells, cavity, planes + 1)
    size = rows // (planes + 1)
    lane_blocks = pl.cdiv(cavity, LANES)
    outside = pl.BlockSpec(memory_space=pltpu.HBM)
    inside = pl.BlockSpec(memory_space=pltpu.VMEM)
    return pl.pallas_call(
        main_kernel,
        in_specs=[outside] * 2
        + [pl.BlockSpec(memory_space=pltpu.SMEM)]
        + [outside] * (3 + len(terms)),
        out_specs=[inside] * 3,
        out_shape=[
            jax.ShapeDtypeStruct((4 * total_freqs, cavity), jnp.bfloat16),
            jax.ShapeDtypeStruct((2, total_freqs, shells), jnp.float32),
            jax.ShapeDtypeStruct(modes.shape, modes.dtype),
        ],
        scratch_shapes=[
            pltpu.VMEM(shell.shape, shell.dtype),
            pltpu.SMEM((slots,), jnp.int32),
            pltpu.VMEM((slots,), jnp.int32),
            pltpu.VMEM((slots,), jnp.float32),
        ]
        + [pltpu.VMEM(term.shape, term.dtype) for term in terms]
        + [
            pltpu.VMEM((depth * lane_blocks, LANES), jnp.float32),
            pltpu.VMEM((slots * lane_blocks, LANES), jnp.float32),
            pltpu.VMEM((shells, slots), jnp.bfloat16),
            pltpu.VMEM((slots, LANES), jnp.float32),
            pltpu.VMEM((rows, LANES), jnp.bfloat16),
            pltpu.VMEM((planes, size, LANES), jnp.bfloat16),
            pltpu.VMEM((size, LANES), jnp.bfloat16),
            pltpu.VMEM((stacks, size, LANES), jnp.bfloat16),
            pltpu.VMEM((rows, LANES), jnp.bfloat16),
            pltpu.SemaphoreType.DMA((CHUNKS,)),
            pltpu.SemaphoreType.DMA((4 + len(terms),)),
            pltpu.SemaphoreType.DMA((3,)),
            pltpu.SemaphoreType.DMA((3,)),
        ],
        compiler_params=pltpu.CompilerParams(
            collective_id=0, has_side_effects=True, vmem_limit_bytes=44 << 20
        ),
    )(
        outer(modes),
        outer(shell),
        count,
        *[outer(value) for value in (fluid_nodes, shell_nodes, area, *terms)],
    )


def field_kernel(amps_ref, modes_ref, structure_ref, pressure_hbm, own_ref, held_ref, out_sem):
    chunk = held_ref.shape[1]
    half = held_ref.shape[2]
    copies = []
    for at in range(held_ref.shape[0]):
        both = jnp.dot(
            amps_ref[...],
            modes_ref[:, at * chunk : (at + 1) * chunk],
            preferred_element_type=jnp.float32,
        )
        held_ref[at] = (both[:half] + both[half:]).T.astype(jnp.bfloat16)
        copies.append(
            pltpu.make_async_copy(
                held_ref.at[at], pressure_hbm.at[pl.ds(at * chunk, chunk)], out_sem.at[at]
            )
        )
        copies[-1].start()
    count = own_ref.shape[1]
    first = pl.multiple_of(lax.axis_index("grp") * count, count)
    own_ref[...] = structure_ref[:, pl.ds(first, count), :]
    for copy in copies:
        copy.wait()


def field(amps, modes, structure, groups):
    depth = modes.shape[1]
    parts, count, shells = structure.shape
    half = amps.shape[0] // 2
    inside = pl.BlockSpec(memory_space=pltpu.VMEM)
    return pl.pallas_call(
        field_kernel,
        in_specs=[inside] * 3,
        out_specs=[pl.BlockSpec(memory_space=pltpu.HBM), inside],
        out_shape=[
            jax.ShapeDtypeStruct((depth, half), jnp.bfloat16),
            jax.ShapeDtypeStruct((parts, count // groups, shells), jnp.float32),
        ],
        scratch_shapes=[
            pltpu.VMEM((CHUNKS, depth // CHUNKS, half), jnp.bfloat16),
            pltpu.SemaphoreType.DMA((CHUNKS,)),
        ],
        compiler_params=pltpu.CompilerParams(vmem_limit_bytes=24 << 20),
    )(amps, modes, structure)


def on_device(acoustic_modes, shell_modes, wet_counts, fluid_nodes, shell_nodes, wet_area, *terms):
    amps, structure, modes = amplitudes(
        acoustic_modes.T,
        shell_modes.T,
        wet_counts,
        fluid_nodes,
        shell_nodes,
        wet_area,
        terms,
        terms[4].shape[0],
    )
    return tuple(field(amps, modes, structure, lax.axis_size("grp")))


def solution(mesh):
    both = P(("fluid", "grp"))
    placed = (P(("fluid", "grp"), None), P("fluid", None)) + (both,) * 4 + (P(),) * 7
    return jax.shard_map(
        on_device,
        mesh=mesh,
        in_specs=placed,
        out_specs=(P(("fluid", "grp"), None), P(None, "grp", None)),
        check_vma=False,
    )
```

```python
import jax
import jax.numpy as jnp
from jax import lax
from jax.experimental import pallas as pl
from jax.experimental.pallas import tpu as pltpu
from jax.sharding import PartitionSpec as P

SECTIONS = 4
MESH = pl.DeviceIdType.MESH
LANES = 128
SIZES = {"z": 8, "xh": 2, "y": 4, "xl": 2, "c": 2}
PLANE = ("xh", "y", "xl", "c")
STACK = ("z",)
CHUNKS = 4
PARTS = 8
TAIL = 4


def offsets_of(names):
    places = [()]
    for name in names:
        places = [place + (step,) for place in places for step in range(SIZES[name])]
    return sorted(places[1:], key=lambda place: -hops(names, place))


def hops(names, place):
    return sum(
        min(step, SIZES[name] - step) for name, step in zip(names, place) if name != "c"
    )


def own_digits():
    fluid, grp = lax.axis_index("fluid"), lax.axis_index("grp")
    digits = {
        "z": fluid // 8,
        "xh": (fluid // 4) % 2,
        "y": fluid % 4,
        "xl": grp // 2,
        "c": grp % 2,
    }
    for name, size in SIZES.items():
        for step in range(1, size):
            digits[name, step] = lax.rem(digits[name] + step, size)
    return digits


def moved(digits, names, offset):
    there = dict(digits)
    for name, step in zip(names, offset):
        if step:
            there[name] = digits[name, step]
    return there


def place_of(digits):
    return (digits["z"] * 8 + digits["xh"] * 4 + digits["y"], digits["xl"] * 2 + digits["c"])


def rank_of(digits, names):
    rank = 0
    for name in names:
        rank = rank * SIZES[name] + digits[name]
    return rank


def column_of(row):
    size = row.shape[1]
    below = lax.broadcasted_iota(jnp.int32, (size, size), 0)
    across = lax.broadcasted_iota(jnp.int32, (size, size), 1)
    spread = jnp.where(below == across, jnp.broadcast_to(row, (size, size)), 0.0)
    return jnp.sum(spread, axis=1, keepdims=True)


def inverse_terms(omega, loss, squared):
    stiff = omega * omega
    real_part = stiff - squared
    imag_part = jnp.broadcast_to(loss * stiff, real_part.shape)
    scale = real_part * real_part + imag_part * imag_part
    return real_part / scale, imag_part / scale


def pad_lanes(values, width):
    if values.shape[1] == width:
        return values
    rest = jnp.zeros((values.shape[0], width - values.shape[1]), values.dtype)
    return jnp.concatenate([values, rest], 1)


def pad_rows(values, height):
    if values.shape[0] == height:
        return values
    rest = jnp.zeros((height - values.shape[0], values.shape[1]), values.dtype)
    return jnp.concatenate([values, rest], 0)


def tail_height(shells):
    return pl.cdiv(pl.cdiv(shells, TAIL), 16) * 16


def rows_needed(shells, cavity, parts):
    high = pl.cdiv(shells, 16) * 16
    used = high * (cavity // LANES) + tail_height(shells)
    return pl.cdiv(used, 16 * parts) * 16 * parts


def pack(total, out_ref):
    shells, cavity = total.shape
    high = pl.cdiv(shells, 16) * 16
    full = cavity // LANES
    for at in range(full):
        piece = pad_rows(total[:, at * LANES : (at + 1) * LANES], high)
        out_ref[pl.ds(at * high, high), :] = piece.astype(out_ref.dtype)
    tall, wide = tail_height(shells), LANES // TAIL
    rest = pad_lanes(pad_rows(total[:, full * LANES :], tall * TAIL), wide)
    tail = jnp.concatenate([rest[at * tall : (at + 1) * tall] for at in range(TAIL)], 1)
    height = out_ref.shape[0] - full * high
    out_ref[pl.ds(full * high, height), :] = pad_rows(tail, height).astype(out_ref.dtype)


def unpack(full_ref, shells, cavity):
    high = pl.cdiv(shells, 16) * 16
    full = cavity // LANES
    tall, wide = tail_height(shells), LANES // TAIL
    blocks = [full_ref[pl.ds(at * high, high), :] for at in range(full)]
    tail = full_ref[pl.ds(full * high, tall), :].astype(jnp.float32)
    rest = [tail[:, at * wide : at * wide + cavity - full * LANES] for at in range(TAIL)]
    rest = jnp.concatenate(rest, 0)[:high].astype(full_ref.dtype)
    return jnp.concatenate(blocks + [rest], 1)[:shells]


def outer(value):
    return pltpu.with_memory_space_constraint(value, pltpu.HBM)


def main_kernel(
    modes_hbm,
    shell_hbm,
    count_ref,
    fluid_hbm,
    node_hbm,
    area_hbm,
    *rest,
):
    terms_hbm = rest[:7]
    amps_ref, structure_ref, modes_ref, free_ref = rest[7:11]
    shell_ref, fluid_ref, node_ref, area_ref = rest[11:15]
    terms = rest[15:22]
    table_ref, rows_ref, pick_ref, area_rows_ref = rest[22:26]
    part_ref, plane_ref, mine_ref, stack_ref, full_ref = rest[26:31]
    modes_sem, small_sem, send_sem, recv_sem = rest[31:]

    cavity, depth = modes_ref.shape
    shells, shell_depth = shell_ref.shape
    slots = fluid_ref.shape[0]
    chunk, span = depth // CHUNKS, slots // PARTS
    lane_blocks = pl.cdiv(cavity, LANES)

    small = [
        pltpu.make_async_copy(source, target, small_sem.at[at])
        for at, (source, target) in enumerate(
            [
                (shell_hbm, shell_ref),
                (node_hbm, node_ref),
                (area_hbm, area_ref),
                (fluid_hbm, fluid_ref),
            ]
            + list(zip(terms_hbm, terms))
        )
    ]
    large = [
        pltpu.make_async_copy(
            modes_hbm.at[:, pl.ds(at * chunk, chunk)],
            modes_ref.at[:, pl.ds(at * chunk, chunk)],
            modes_sem.at[at],
        )
        for at in range(CHUNKS)
    ]
    for copy in large[:1] + small + large[1:]:
        copy.start()

    digits = own_digits()
    plane, stack = offsets_of(PLANE), offsets_of(STACK)
    barrier = pltpu.get_barrier_semaphore()
    for names, offsets in ((PLANE, plane), (STACK, stack)):
        for offset in offsets:
            pl.semaphore_signal(
                barrier,
                inc=1,
                device_id=place_of(moved(digits, names, offset)),
                device_id_type=MESH,
            )

    for at in range(CHUNKS):
        large[at].wait()
        for block in range(lane_blocks):
            first = block * LANES
            wide = min(LANES, cavity - first)
            piece = modes_ref[first : first + wide, at * chunk : (at + 1) * chunk].T
            table_ref[pl.ds(at * chunk * lane_blocks + block, chunk, stride=lane_blocks), :] = (
                pad_lanes(piece.astype(jnp.float32), LANES)
            )
    for copy in small:
        copy.wait()
    count = count_ref[0]
    for at in range(PARTS):
        here = pl.ds(at * span, span)
        area_rows_ref[here, :] = jnp.broadcast_to(
            area_ref[here].reshape(1, span), (LANES, span)
        ).T

    def gather(step, carry):
        here = pl.ds(pl.multiple_of(step * span, span), span)
        slot = lax.broadcasted_iota(jnp.int32, (1, span), 1) + step * span
        node = jnp.where(slot < count, node_ref[here].reshape(1, span), -1)
        number = lax.broadcasted_iota(jnp.int32, (shell_depth, span), 0)
        hot = jnp.where(number == node, 1.0, 0.0).astype(jnp.bfloat16)
        pick_ref[:, here] = jnp.dot(
            shell_ref[...], hot, preferred_element_type=jnp.float32
        ).astype(jnp.bfloat16)
        for at in range(span):
            row = step * span + at
            rows_ref[pl.ds(pl.multiple_of(row * lane_blocks, lane_blocks), lane_blocks), :] = (
                table_ref[pl.ds(fluid_ref[row] * lane_blocks, lane_blocks), :]
            )
        return carry

    lax.fori_loop(0, PARTS, gather, 0)
    area = area_rows_ref[...]
    wet = jnp.concatenate(
        [
            (rows_ref[pl.ds(block, slots, stride=lane_blocks), :] * area).astype(jnp.bfloat16)
            for block in range(lane_blocks)
        ],
        1,
    )
    total = jnp.dot(pick_ref[...], wet, preferred_element_type=jnp.float32)
    pack(total[:, :cavity], part_ref)

    size = mine_ref.shape[0]
    own = rank_of(digits, PLANE)

    def rows_of(rank):
        return pl.ds(pl.multiple_of(rank * size, size), size)

    pl.semaphore_wait(barrier, len(plane) + len(stack))
    for slot, offset in enumerate(plane):
        there = moved(digits, PLANE, offset)
        pltpu.make_async_remote_copy(
            src_ref=part_ref.at[rows_of(rank_of(there, PLANE))],
            dst_ref=plane_ref.at[slot],
            send_sem=send_sem.at[0],
            recv_sem=recv_sem.at[0],
            device_id=place_of(there),
            device_id_type=MESH,
        ).start()

    shell_freq, shell_loss, cavity_freq, cavity_loss, freqs, force, source = [
        term[...].reshape(1, term.shape[0]) for term in terms
    ]
    frequencies = column_of(freqs)
    squared = frequencies * frequencies
    shell_p, shell_q = inverse_terms(shell_freq, shell_loss, squared)
    cavity_p, cavity_q = inverse_terms(cavity_freq, cavity_loss, squared)
    base_re = source * cavity_p
    base_im = -source * cavity_q
    back_p, back_q = squared * cavity_p, squared * cavity_q

    pltpu.make_async_copy(plane_ref, plane_ref, recv_sem.at[0]).wait()
    mine_ref[...] = (
        part_ref[rows_of(own), :].astype(jnp.float32)
        + jnp.sum(plane_ref[...].astype(jnp.float32), axis=0)
    ).astype(jnp.bfloat16)

    for slot, offset in enumerate(stack):
        pltpu.make_async_remote_copy(
            src_ref=mine_ref,
            dst_ref=stack_ref.at[slot],
            send_sem=send_sem.at[1],
            recv_sem=recv_sem.at[1],
            device_id=place_of(moved(digits, STACK, offset)),
            device_id_type=MESH,
        ).start()

    free = jnp.concatenate([base_re, base_im], 0).astype(jnp.bfloat16)
    for at in range(PARTS):
        here = pl.ds(at * (depth // PARTS), depth // PARTS)
        free_ref[:, here] = jnp.dot(free, modes_ref[:, here], preferred_element_type=jnp.float32)

    pltpu.make_async_copy(stack_ref, stack_ref, recv_sem.at[1]).wait()
    full_ref[rows_of(own), :] = (
        mine_ref[...].astype(jnp.float32)
        + jnp.sum(stack_ref[...].astype(jnp.float32), axis=0)
    ).astype(jnp.bfloat16)

    for offset in plane:
        pltpu.make_async_remote_copy(
            src_ref=full_ref.at[rows_of(own)],
            dst_ref=full_ref.at[rows_of(own)],
            send_sem=send_sem.at[2],
            recv_sem=recv_sem.at[2],
            device_id=place_of(moved(digits, PLANE, offset)),
            device_id_type=MESH,
        ).start()
    pltpu.make_async_copy(plane_ref, plane_ref, recv_sem.at[2]).wait()

    coupling = unpack(full_ref, shells, cavity)
    total_freqs = squared.shape[0]
    real, imag = base_re, base_im
    for section in range(SECTIONS):
        loads = lax.dot_general(
            jnp.concatenate([real, imag], 0).astype(jnp.bfloat16),
            coupling,
            (((1,), (1,)), ((), ())),
            preferred_element_type=jnp.float32,
        )
        load_re, load_im = force + loads[:total_freqs], loads[total_freqs:]
        struct_re = load_re * shell_p + load_im * shell_q
        struct_im = load_im * shell_p - load_re * shell_q
        back = jnp.dot(
            jnp.concatenate([struct_re, struct_im], 0).astype(jnp.bfloat16),
            coupling,
            preferred_element_type=jnp.float32,
        )
        back_re, back_im = back[:total_freqs], back[total_freqs:]
        coupled_re = back_re * back_p + back_im * back_q
        coupled_im = back_im * back_p - back_re * back_q
        real, imag = base_re + coupled_re, base_im + coupled_im
    amps_ref[pl.ds(0, total_freqs), :] = coupled_re.astype(jnp.bfloat16)
    amps_ref[pl.ds(total_freqs, total_freqs), :] = coupled_im.astype(jnp.bfloat16)
    structure_ref[0] = struct_re
    structure_ref[1] = struct_im

    pltpu.make_async_copy(plane_ref, plane_ref, send_sem.at[0]).wait()
    pltpu.make_async_copy(stack_ref, stack_ref, send_sem.at[1]).wait()
    pltpu.make_async_copy(plane_ref, plane_ref, send_sem.at[2]).wait()


def amplitudes(modes, shell, count, fluid_nodes, shell_nodes, area, terms, total_freqs):
    cavity, depth = modes.shape
    shells = shell.shape[0]
    slots = fluid_nodes.shape[0]
    planes, stacks = len(offsets_of(PLANE)), len(offsets_of(STACK))
    rows = rows_needed(shells, cavity, planes + 1)
    size = rows // (planes + 1)
    lane_blocks = pl.cdiv(cavity, LANES)
    outside = pl.BlockSpec(memory_space=pltpu.HBM)
    inside = pl.BlockSpec(memory_space=pltpu.VMEM)
    return pl.pallas_call(
        main_kernel,
        in_specs=[outside] * 2
        + [pl.BlockSpec(memory_space=pltpu.SMEM)]
        + [outside] * (3 + len(terms)),
        out_specs=[inside] * 4,
        out_shape=[
            jax.ShapeDtypeStruct((2 * total_freqs, cavity), jnp.bfloat16),
            jax.ShapeDtypeStruct((2, total_freqs, shells), jnp.float32),
            jax.ShapeDtypeStruct(modes.shape, modes.dtype),
            jax.ShapeDtypeStruct((2 * total_freqs, depth), jnp.float32),
        ],
        scratch_shapes=[
            pltpu.VMEM(shell.shape, shell.dtype),
            pltpu.SMEM((slots,), jnp.int32),
            pltpu.VMEM((slots,), jnp.int32),
            pltpu.VMEM((slots,), jnp.float32),
        ]
        + [pltpu.VMEM(term.shape, term.dtype) for term in terms]
        + [
            pltpu.VMEM((depth * lane_blocks, LANES), jnp.float32),
            pltpu.VMEM((slots * lane_blocks, LANES), jnp.float32),
            pltpu.VMEM((shells, slots), jnp.bfloat16),
            pltpu.VMEM((slots, LANES), jnp.float32),
            pltpu.VMEM((rows, LANES), jnp.bfloat16),
            pltpu.VMEM((planes, size, LANES), jnp.bfloat16),
            pltpu.VMEM((size, LANES), jnp.bfloat16),
            pltpu.VMEM((stacks, size, LANES), jnp.bfloat16),
            pltpu.VMEM((rows, LANES), jnp.bfloat16),
            pltpu.SemaphoreType.DMA((CHUNKS,)),
            pltpu.SemaphoreType.DMA((4 + len(terms),)),
            pltpu.SemaphoreType.DMA((3,)),
            pltpu.SemaphoreType.DMA((3,)),
        ],
        compiler_params=pltpu.CompilerParams(
            collective_id=0, has_side_effects=True, vmem_limit_bytes=44 << 20
        ),
    )(
        outer(modes),
        outer(shell),
        count,
        *[outer(value) for value in (fluid_nodes, shell_nodes, area, *terms)],
    )


def field_kernel(
    amps_ref, modes_ref, free_ref, structure_ref, pressure_hbm, own_ref, held_ref, out_sem
):
    chunk = held_ref.shape[1]
    copies = []
    for at in range(held_ref.shape[0]):
        here = pl.ds(at * chunk, chunk)
        coupled = jnp.dot(
            amps_ref[...], modes_ref[:, here], preferred_element_type=jnp.float32
        )
        held_ref[at] = (free_ref[:, here] + coupled).T.astype(jnp.bfloat16)
        copies.append(
            pltpu.make_async_copy(held_ref.at[at], pressure_hbm.at[here], out_sem.at[at])
        )
        copies[-1].start()
    count = own_ref.shape[1]
    first = pl.multiple_of(lax.axis_index("grp") * count, count)
    own_ref[...] = structure_ref[:, pl.ds(first, count), :]
    for copy in copies:
        copy.wait()


def field(amps, modes, free, structure, groups):
    depth = modes.shape[1]
    parts, count, shells = structure.shape
    half = amps.shape[0]
    inside = pl.BlockSpec(memory_space=pltpu.VMEM)
    return pl.pallas_call(
        field_kernel,
        in_specs=[inside] * 4,
        out_specs=[pl.BlockSpec(memory_space=pltpu.HBM), inside],
        out_shape=[
            jax.ShapeDtypeStruct((depth, half), jnp.bfloat16),
            jax.ShapeDtypeStruct((parts, count // groups, shells), jnp.float32),
        ],
        scratch_shapes=[
            pltpu.VMEM((PARTS, depth // PARTS, half), jnp.bfloat16),
            pltpu.SemaphoreType.DMA((PARTS,)),
        ],
        compiler_params=pltpu.CompilerParams(vmem_limit_bytes=24 << 20),
    )(amps, modes, free, structure)


def on_device(acoustic_modes, shell_modes, wet_counts, fluid_nodes, shell_nodes, wet_area, *terms):
    amps, structure, modes, free = amplitudes(
        acoustic_modes.T,
        shell_modes.T,
        wet_counts,
        fluid_nodes,
        shell_nodes,
        wet_area,
        terms,
        terms[4].shape[0],
    )
    return tuple(field(amps, modes, free, structure, lax.axis_size("grp")))


def solution(mesh):
    both = P(("fluid", "grp"))
    placed = (P(("fluid", "grp"), None), P("fluid", None)) + (both,) * 4 + (P(),) * 7
    return jax.shard_map(
        on_device,
        mesh=mesh,
        in_specs=placed,
        out_specs=(P(("fluid", "grp"), None), P(None, "grp", None)),
        check_vma=False,
    )
```

```python
import jax
import jax.numpy as jnp
from jax import lax
from jax.experimental import pallas as pl
from jax.experimental.pallas import tpu as pltpu
from jax.sharding import PartitionSpec as P

SECTIONS = 4
MESH = pl.DeviceIdType.MESH
LANES = 128
SIZES = {"z": 8, "xh": 2, "y": 4, "xl": 2, "c": 2}
PLANE = ("xh", "y", "xl", "c")
STACK = ("z",)
CHUNKS = 4
PARTS = 8
TAIL = 4


def offsets_of(names):
    places = [()]
    for name in names:
        places = [place + (step,) for place in places for step in range(SIZES[name])]
    return sorted(places[1:], key=lambda place: -hops(names, place))


def hops(names, place):
    return sum(
        min(step, SIZES[name] - step) for name, step in zip(names, place) if name != "c"
    )


def own_digits():
    fluid, grp = lax.axis_index("fluid"), lax.axis_index("grp")
    digits = {
        "z": fluid // 8,
        "xh": (fluid // 4) % 2,
        "y": fluid % 4,
        "xl": grp // 2,
        "c": grp % 2,
    }
    for name, size in SIZES.items():
        for step in range(1, size):
            digits[name, step] = lax.rem(digits[name] + step, size)
    return digits


def moved(digits, names, offset):
    there = dict(digits)
    for name, step in zip(names, offset):
        if step:
            there[name] = digits[name, step]
    return there


def place_of(digits):
    return (digits["z"] * 8 + digits["xh"] * 4 + digits["y"], digits["xl"] * 2 + digits["c"])


def rank_of(digits, names):
    rank = 0
    for name in names:
        rank = rank * SIZES[name] + digits[name]
    return rank


def column_of(row):
    size = row.shape[1]
    below = lax.broadcasted_iota(jnp.int32, (size, size), 0)
    across = lax.broadcasted_iota(jnp.int32, (size, size), 1)
    spread = jnp.where(below == across, jnp.broadcast_to(row, (size, size)), 0.0)
    return jnp.sum(spread, axis=1, keepdims=True)


def inverse_terms(omega, loss, squared):
    stiff = omega * omega
    real_part = stiff - squared
    imag_part = jnp.broadcast_to(loss * stiff, real_part.shape)
    scale = real_part * real_part + imag_part * imag_part
    return real_part / scale, imag_part / scale


def pad_lanes(values, width):
    if values.shape[1] == width:
        return values
    rest = jnp.zeros((values.shape[0], width - values.shape[1]), values.dtype)
    return jnp.concatenate([values, rest], 1)


def pad_rows(values, height):
    if values.shape[0] == height:
        return values
    rest = jnp.zeros((height - values.shape[0], values.shape[1]), values.dtype)
    return jnp.concatenate([values, rest], 0)


def tail_height(shells):
    return pl.cdiv(pl.cdiv(shells, TAIL), 16) * 16


def rows_needed(shells, cavity, parts):
    high = pl.cdiv(shells, 16) * 16
    used = high * (cavity // LANES) + tail_height(shells)
    return pl.cdiv(used, 16 * parts) * 16 * parts


def pack(total, out_ref):
    shells, cavity = total.shape
    high = pl.cdiv(shells, 16) * 16
    full = cavity // LANES
    for at in range(full):
        piece = pad_rows(total[:, at * LANES : (at + 1) * LANES], high)
        out_ref[pl.ds(at * high, high), :] = piece.astype(out_ref.dtype)
    tall, wide = tail_height(shells), LANES // TAIL
    rest = pad_lanes(pad_rows(total[:, full * LANES :], tall * TAIL), wide)
    tail = jnp.concatenate([rest[at * tall : (at + 1) * tall] for at in range(TAIL)], 1)
    height = out_ref.shape[0] - full * high
    out_ref[pl.ds(full * high, height), :] = pad_rows(tail, height).astype(out_ref.dtype)


def unpack(full_ref, shells, cavity):
    high = pl.cdiv(shells, 16) * 16
    full = cavity // LANES
    tall, wide = tail_height(shells), LANES // TAIL
    blocks = [full_ref[pl.ds(at * high, high), :] for at in range(full)]
    tail = full_ref[pl.ds(full * high, tall), :].astype(jnp.float32)
    rest = [tail[:, at * wide : at * wide + cavity - full * LANES] for at in range(TAIL)]
    rest = jnp.concatenate(rest, 0)[:high].astype(full_ref.dtype)
    return jnp.concatenate(blocks + [rest], 1)[:shells]


def outer(value):
    return pltpu.with_memory_space_constraint(value, pltpu.HBM)


def main_kernel(
    modes_hbm,
    shell_hbm,
    count_ref,
    fluid_hbm,
    node_hbm,
    area_hbm,
    *rest,
):
    terms_hbm = rest[:7]
    amps_ref, structure_ref, modes_ref, free_ref = rest[7:11]
    shell_ref, fluid_ref, node_ref, area_ref = rest[11:15]
    terms = rest[15:22]
    table_ref, rows_ref, pick_ref, area_rows_ref = rest[22:26]
    part_ref, plane_ref, mine_ref, stack_ref, full_ref = rest[26:31]
    modes_sem, small_sem, send_sem, recv_sem = rest[31:]

    cavity, depth = modes_ref.shape
    shells, shell_depth = shell_ref.shape
    slots = fluid_ref.shape[0]
    chunk, span = depth // CHUNKS, slots // PARTS
    lane_blocks = pl.cdiv(cavity, LANES)

    small = [
        pltpu.make_async_copy(source, target, small_sem.at[at])
        for at, (source, target) in enumerate(
            [
                (shell_hbm, shell_ref),
                (node_hbm, node_ref),
                (area_hbm, area_ref),
                (fluid_hbm, fluid_ref),
            ]
            + list(zip(terms_hbm, terms))
        )
    ]
    large = [
        pltpu.make_async_copy(
            modes_hbm.at[:, pl.ds(at * chunk, chunk)],
            modes_ref.at[:, pl.ds(at * chunk, chunk)],
            modes_sem.at[at],
        )
        for at in range(CHUNKS)
    ]
    for copy in large[:1] + small + large[1:]:
        copy.start()

    digits = own_digits()
    plane, stack = offsets_of(PLANE), offsets_of(STACK)
    barrier = pltpu.get_barrier_semaphore()
    for names, offsets in ((PLANE, plane), (STACK, stack)):
        for offset in offsets:
            pl.semaphore_signal(
                barrier,
                inc=1,
                device_id=place_of(moved(digits, names, offset)),
                device_id_type=MESH,
            )

    for at in range(CHUNKS):
        large[at].wait()
        for block in range(lane_blocks):
            first = block * LANES
            wide = min(LANES, cavity - first)
            piece = modes_ref[first : first + wide, at * chunk : (at + 1) * chunk].T
            table_ref[pl.ds(at * chunk * lane_blocks + block, chunk, stride=lane_blocks), :] = (
                pad_lanes(piece.astype(jnp.float32), LANES)
            )
    for copy in small:
        copy.wait()
    count = count_ref[0]
    for at in range(PARTS):
        here = pl.ds(at * span, span)
        area_rows_ref[here, :] = jnp.broadcast_to(
            area_ref[here].reshape(1, span), (LANES, span)
        ).T

    def gather(step, carry):
        here = pl.ds(pl.multiple_of(step * span, span), span)
        slot = lax.broadcasted_iota(jnp.int32, (1, span), 1) + step * span
        node = jnp.where(slot < count, node_ref[here].reshape(1, span), -1)
        number = lax.broadcasted_iota(jnp.int32, (shell_depth, span), 0)
        hot = jnp.where(number == node, 1.0, 0.0).astype(jnp.bfloat16)
        pick_ref[:, here] = jnp.dot(
            shell_ref[...], hot, preferred_element_type=jnp.float32
        ).astype(jnp.bfloat16)
        for at in range(span):
            row = step * span + at
            rows_ref[pl.ds(pl.multiple_of(row * lane_blocks, lane_blocks), lane_blocks), :] = (
                table_ref[pl.ds(fluid_ref[row] * lane_blocks, lane_blocks), :]
            )
        return carry

    lax.fori_loop(0, PARTS, gather, 0)
    area = area_rows_ref[...]
    wet = jnp.concatenate(
        [
            (rows_ref[pl.ds(block, slots, stride=lane_blocks), :] * area).astype(jnp.bfloat16)
            for block in range(lane_blocks)
        ],
        1,
    )
    total = jnp.dot(pick_ref[...], wet, preferred_element_type=jnp.float32)
    pack(total[:, :cavity], part_ref)

    size = mine_ref.shape[0]
    own = rank_of(digits, PLANE)

    def rows_of(rank):
        return pl.ds(pl.multiple_of(rank * size, size), size)

    pl.semaphore_wait(barrier, len(plane) + len(stack))
    for slot, offset in enumerate(plane):
        there = moved(digits, PLANE, offset)
        pltpu.make_async_remote_copy(
            src_ref=part_ref.at[rows_of(rank_of(there, PLANE))],
            dst_ref=plane_ref.at[slot],
            send_sem=send_sem.at[0],
            recv_sem=recv_sem.at[0],
            device_id=place_of(there),
            device_id_type=MESH,
        ).start()

    shell_freq, shell_loss, cavity_freq, cavity_loss, freqs, force, source = [
        term[...].reshape(1, term.shape[0]) for term in terms
    ]
    frequencies = column_of(freqs)
    squared = frequencies * frequencies
    shell_p, shell_q = inverse_terms(shell_freq, shell_loss, squared)
    cavity_p, cavity_q = inverse_terms(cavity_freq, cavity_loss, squared)
    base_re = source * cavity_p
    base_im = -source * cavity_q
    back_p, back_q = squared * cavity_p, squared * cavity_q

    pltpu.make_async_copy(plane_ref, plane_ref, recv_sem.at[0]).wait()
    mine_ref[...] = (
        part_ref[rows_of(own), :].astype(jnp.float32)
        + jnp.sum(plane_ref[...].astype(jnp.float32), axis=0)
    ).astype(jnp.bfloat16)

    for slot, offset in enumerate(stack):
        pltpu.make_async_remote_copy(
            src_ref=mine_ref,
            dst_ref=stack_ref.at[slot],
            send_sem=send_sem.at[1],
            recv_sem=recv_sem.at[1],
            device_id=place_of(moved(digits, STACK, offset)),
            device_id_type=MESH,
        ).start()

    free = jnp.concatenate([base_re, base_im], 0).astype(jnp.bfloat16)
    for at in range(PARTS):
        here = pl.ds(at * (depth // PARTS), depth // PARTS)
        free_ref[:, here] = jnp.dot(free, modes_ref[:, here], preferred_element_type=jnp.float32)

    pltpu.make_async_copy(stack_ref, stack_ref, recv_sem.at[1]).wait()
    full_ref[rows_of(own), :] = (
        mine_ref[...].astype(jnp.float32)
        + jnp.sum(stack_ref[...].astype(jnp.float32), axis=0)
    ).astype(jnp.bfloat16)

    for offset in plane:
        pltpu.make_async_remote_copy(
            src_ref=full_ref.at[rows_of(own)],
            dst_ref=full_ref.at[rows_of(own)],
            send_sem=send_sem.at[2],
            recv_sem=recv_sem.at[2],
            device_id=place_of(moved(digits, PLANE, offset)),
            device_id_type=MESH,
        ).start()
    pltpu.make_async_copy(plane_ref, plane_ref, recv_sem.at[2]).wait()

    coupling = unpack(full_ref, shells, cavity)
    total_freqs = squared.shape[0]
    real, imag = base_re, base_im
    for section in range(SECTIONS):
        loads = lax.dot_general(
            jnp.concatenate([real, imag], 0).astype(jnp.bfloat16),
            coupling,
            (((1,), (1,)), ((), ())),
            preferred_element_type=jnp.float32,
        )
        load_re, load_im = force + loads[:total_freqs], loads[total_freqs:]
        struct_re = load_re * shell_p + load_im * shell_q
        struct_im = load_im * shell_p - load_re * shell_q
        back = jnp.dot(
            jnp.concatenate([struct_re, struct_im], 0).astype(jnp.bfloat16),
            coupling,
            preferred_element_type=jnp.float32,
        )
        back_re, back_im = back[:total_freqs], back[total_freqs:]
        coupled_re = back_re * back_p + back_im * back_q
        coupled_im = back_im * back_p - back_re * back_q
        real, imag = base_re + coupled_re, base_im + coupled_im
    amps_ref[pl.ds(0, total_freqs), :] = coupled_re.astype(jnp.bfloat16)
    amps_ref[pl.ds(total_freqs, total_freqs), :] = coupled_im.astype(jnp.bfloat16)
    structure_ref[0] = struct_re
    structure_ref[1] = struct_im

    pltpu.make_async_copy(plane_ref, plane_ref, send_sem.at[0]).wait()
    pltpu.make_async_copy(stack_ref, stack_ref, send_sem.at[1]).wait()
    pltpu.make_async_copy(plane_ref, plane_ref, send_sem.at[2]).wait()


def amplitudes(modes, shell, count, fluid_nodes, shell_nodes, area, terms, total_freqs):
    cavity, depth = modes.shape
    shells = shell.shape[0]
    slots = fluid_nodes.shape[0]
    planes, stacks = len(offsets_of(PLANE)), len(offsets_of(STACK))
    rows = rows_needed(shells, cavity, planes + 1)
    size = rows // (planes + 1)
    lane_blocks = pl.cdiv(cavity, LANES)
    outside = pl.BlockSpec(memory_space=pltpu.HBM)
    inside = pl.BlockSpec(memory_space=pltpu.VMEM)
    return pl.pallas_call(
        main_kernel,
        in_specs=[outside] * 2
        + [pl.BlockSpec(memory_space=pltpu.SMEM)]
        + [outside] * (3 + len(terms)),
        out_specs=[inside] * 4,
        out_shape=[
            jax.ShapeDtypeStruct((2 * total_freqs, cavity), jnp.bfloat16),
            jax.ShapeDtypeStruct((2, total_freqs, shells), jnp.float32),
            jax.ShapeDtypeStruct(modes.shape, modes.dtype),
            jax.ShapeDtypeStruct((2 * total_freqs, depth), jnp.float32),
        ],
        scratch_shapes=[
            pltpu.VMEM(shell.shape, shell.dtype),
            pltpu.SMEM((slots,), jnp.int32),
            pltpu.VMEM((slots,), jnp.int32),
            pltpu.VMEM((slots,), jnp.float32),
        ]
        + [pltpu.VMEM(term.shape, term.dtype) for term in terms]
        + [
            pltpu.VMEM((depth * lane_blocks, LANES), jnp.float32),
            pltpu.VMEM((slots * lane_blocks, LANES), jnp.float32),
            pltpu.VMEM((shells, slots), jnp.bfloat16),
            pltpu.VMEM((slots, LANES), jnp.float32),
            pltpu.VMEM((rows, LANES), jnp.bfloat16),
            pltpu.VMEM((planes, size, LANES), jnp.bfloat16),
            pltpu.VMEM((size, LANES), jnp.bfloat16),
            pltpu.VMEM((stacks, size, LANES), jnp.bfloat16),
            pltpu.VMEM((rows, LANES), jnp.bfloat16),
            pltpu.SemaphoreType.DMA((CHUNKS,)),
            pltpu.SemaphoreType.DMA((4 + len(terms),)),
            pltpu.SemaphoreType.DMA((3,)),
            pltpu.SemaphoreType.DMA((3,)),
        ],
        compiler_params=pltpu.CompilerParams(
            collective_id=0, has_side_effects=True, vmem_limit_bytes=34 << 20
        ),
    )(
        outer(modes),
        outer(shell),
        count,
        *[outer(value) for value in (fluid_nodes, shell_nodes, area, *terms)],
    )


def field_kernel(
    amps_ref, modes_ref, free_ref, structure_ref, pressure_hbm, own_ref, held_ref, out_sem
):
    chunk = held_ref.shape[1]
    copies = []
    for at in range(held_ref.shape[0]):
        here = pl.ds(at * chunk, chunk)
        coupled = jnp.dot(
            amps_ref[...], modes_ref[:, here], preferred_element_type=jnp.float32
        )
        held_ref[at] = (free_ref[:, here] + coupled).T.astype(jnp.bfloat16)
        copies.append(
            pltpu.make_async_copy(held_ref.at[at], pressure_hbm.at[here], out_sem.at[at])
        )
        copies[-1].start()
    count = own_ref.shape[1]
    first = pl.multiple_of(lax.axis_index("grp") * count, count)
    own_ref[...] = structure_ref[:, pl.ds(first, count), :]
    for copy in copies:
        copy.wait()


def field(amps, modes, free, structure, groups):
    depth = modes.shape[1]
    parts, count, shells = structure.shape
    half = amps.shape[0]
    inside = pl.BlockSpec(memory_space=pltpu.VMEM)
    return pl.pallas_call(
        field_kernel,
        in_specs=[inside] * 4,
        out_specs=[pl.BlockSpec(memory_space=pltpu.HBM), inside],
        out_shape=[
            jax.ShapeDtypeStruct((depth, half), jnp.bfloat16),
            jax.ShapeDtypeStruct((parts, count // groups, shells), jnp.float32),
        ],
        scratch_shapes=[
            pltpu.VMEM((PARTS, depth // PARTS, half), jnp.bfloat16),
            pltpu.SemaphoreType.DMA((PARTS,)),
        ],
        compiler_params=pltpu.CompilerParams(vmem_limit_bytes=16 << 20),
    )(amps, modes, free, structure)


def on_device(acoustic_modes, shell_modes, wet_counts, fluid_nodes, shell_nodes, wet_area, *terms):
    amps, structure, modes, free = amplitudes(
        acoustic_modes.T,
        shell_modes.T,
        wet_counts,
        fluid_nodes,
        shell_nodes,
        wet_area,
        terms,
        terms[4].shape[0],
    )
    return tuple(field(amps, modes, free, structure, lax.axis_size("grp")))


def solution(mesh):
    both = P(("fluid", "grp"))
    placed = (P(("fluid", "grp"), None), P("fluid", None)) + (both,) * 4 + (P(),) * 7
    return jax.shard_map(
        on_device,
        mesh=mesh,
        in_specs=placed,
        out_specs=(P(("fluid", "grp"), None), P(None, "grp", None)),
        check_vma=False,
    )
```

```python
import jax
import jax.numpy as jnp
from jax import lax
from jax.experimental import pallas as pl
from jax.experimental.pallas import tpu as pltpu
from jax.sharding import PartitionSpec as P

SECTIONS = 4
MESH = pl.DeviceIdType.MESH
LANES = 128
SIZES = {"z": 8, "xh": 2, "y": 4, "xl": 2, "c": 2}
PLANE = ("xh", "y", "xl", "c")
STACK = ("z",)
CHUNKS = 4
PARTS = 8
STEPS = 4
TAIL = 4


def offsets_of(names):
    places = [()]
    for name in names:
        places = [place + (step,) for place in places for step in range(SIZES[name])]
    return sorted(places[1:], key=lambda place: -hops(names, place))


def hops(names, place):
    return sum(
        min(step, SIZES[name] - step) for name, step in zip(names, place) if name != "c"
    )


def own_digits():
    fluid, grp = lax.axis_index("fluid"), lax.axis_index("grp")
    digits = {
        "z": fluid // 8,
        "xh": (fluid // 4) % 2,
        "y": fluid % 4,
        "xl": grp // 2,
        "c": grp % 2,
    }
    for name, size in SIZES.items():
        for step in range(1, size):
            digits[name, step] = lax.rem(digits[name] + step, size)
    return digits


def moved(digits, names, offset):
    there = dict(digits)
    for name, step in zip(names, offset):
        if step:
            there[name] = digits[name, step]
    return there


def place_of(digits):
    return (digits["z"] * 8 + digits["xh"] * 4 + digits["y"], digits["xl"] * 2 + digits["c"])


def rank_of(digits, names):
    rank = 0
    for name in names:
        rank = rank * SIZES[name] + digits[name]
    return rank


def column_of(row):
    size = row.shape[1]
    below = lax.broadcasted_iota(jnp.int32, (size, size), 0)
    across = lax.broadcasted_iota(jnp.int32, (size, size), 1)
    spread = jnp.where(below == across, jnp.broadcast_to(row, (size, size)), 0.0)
    return jnp.sum(spread, axis=1, keepdims=True)


def inverse_terms(omega, loss, squared):
    stiff = omega * omega
    real_part = stiff - squared
    imag_part = jnp.broadcast_to(loss * stiff, real_part.shape)
    scale = real_part * real_part + imag_part * imag_part
    return real_part / scale, imag_part / scale


def pad_lanes(values, width):
    if values.shape[1] == width:
        return values
    rest = jnp.zeros((values.shape[0], width - values.shape[1]), values.dtype)
    return jnp.concatenate([values, rest], 1)


def pad_rows(values, height):
    if values.shape[0] == height:
        return values
    rest = jnp.zeros((height - values.shape[0], values.shape[1]), values.dtype)
    return jnp.concatenate([values, rest], 0)


def tail_height(shells):
    return pl.cdiv(pl.cdiv(shells, TAIL), 16) * 16


def rows_needed(shells, cavity, parts):
    high = pl.cdiv(shells, 16) * 16
    used = high * (cavity // LANES) + tail_height(shells)
    return pl.cdiv(used, 16 * parts) * 16 * parts


def pack(total, out_ref):
    shells, cavity = total.shape
    high = pl.cdiv(shells, 16) * 16
    full = cavity // LANES
    for at in range(full):
        piece = pad_rows(total[:, at * LANES : (at + 1) * LANES], high)
        out_ref[pl.ds(at * high, high), :] = piece.astype(out_ref.dtype)
    tall, wide = tail_height(shells), LANES // TAIL
    rest = pad_lanes(pad_rows(total[:, full * LANES :], tall * TAIL), wide)
    tail = jnp.concatenate([rest[at * tall : (at + 1) * tall] for at in range(TAIL)], 1)
    height = out_ref.shape[0] - full * high
    out_ref[pl.ds(full * high, height), :] = pad_rows(tail, height).astype(out_ref.dtype)


def unpack(full_ref, shells, cavity):
    high = pl.cdiv(shells, 16) * 16
    full = cavity // LANES
    tall, wide = tail_height(shells), LANES // TAIL
    blocks = [full_ref[pl.ds(at * high, high), :] for at in range(full)]
    tail = full_ref[pl.ds(full * high, tall), :].astype(jnp.float32)
    rest = [tail[:, at * wide : at * wide + cavity - full * LANES] for at in range(TAIL)]
    rest = jnp.concatenate(rest, 0)[:high].astype(full_ref.dtype)
    return jnp.concatenate(blocks + [rest], 1)[:shells]


def outer(value):
    return pltpu.with_memory_space_constraint(value, pltpu.HBM)


def main_kernel(
    modes_hbm,
    shell_hbm,
    count_ref,
    fluid_hbm,
    node_hbm,
    area_hbm,
    *rest,
):
    terms_hbm = rest[:7]
    amps_ref, structure_ref, modes_ref, free_ref = rest[7:11]
    shell_ref, fluid_ref, node_ref, area_ref = rest[11:15]
    terms = rest[15:22]
    table_ref, rows_ref, pick_ref, area_rows_ref = rest[22:26]
    part_ref, plane_ref, mine_ref, stack_ref, full_ref = rest[26:31]
    modes_sem, small_sem, send_sem, recv_sem = rest[31:]

    cavity, depth = modes_ref.shape
    shells, shell_depth = shell_ref.shape
    slots = fluid_ref.shape[0]
    chunk, span = depth // CHUNKS, slots // STEPS
    lane_blocks = pl.cdiv(cavity, LANES)

    small = [
        pltpu.make_async_copy(source, target, small_sem.at[at])
        for at, (source, target) in enumerate(
            [
                (shell_hbm, shell_ref),
                (node_hbm, node_ref),
                (area_hbm, area_ref),
                (fluid_hbm, fluid_ref),
            ]
            + list(zip(terms_hbm, terms))
        )
    ]
    large = [
        pltpu.make_async_copy(
            modes_hbm.at[:, pl.ds(at * chunk, chunk)],
            modes_ref.at[:, pl.ds(at * chunk, chunk)],
            modes_sem.at[at],
        )
        for at in range(CHUNKS)
    ]
    for copy in large[:1] + small + large[1:]:
        copy.start()

    digits = own_digits()
    plane, stack = offsets_of(PLANE), offsets_of(STACK)
    barrier = pltpu.get_barrier_semaphore()
    for names, offsets in ((PLANE, plane), (STACK, stack)):
        for offset in offsets:
            pl.semaphore_signal(
                barrier,
                inc=1,
                device_id=place_of(moved(digits, names, offset)),
                device_id_type=MESH,
            )

    for at in range(CHUNKS):
        large[at].wait()
        for block in range(lane_blocks):
            first = block * LANES
            wide = min(LANES, cavity - first)
            piece = modes_ref[first : first + wide, at * chunk : (at + 1) * chunk].T
            table_ref[pl.ds(at * chunk * lane_blocks + block, chunk, stride=lane_blocks), :] = (
                pad_lanes(piece.astype(jnp.float32), LANES)
            )
    for copy in small:
        copy.wait()
    count = count_ref[0]

    def gather(step, carry):
        here = pl.ds(pl.multiple_of(step * span, span), span)
        slot = lax.broadcasted_iota(jnp.int32, (1, span), 1) + step * span
        node = jnp.where(slot < count, node_ref[here].reshape(1, span), -1)
        number = lax.broadcasted_iota(jnp.int32, (shell_depth, span), 0)
        hot = jnp.where(number == node, 1.0, 0.0).astype(jnp.bfloat16)
        pick_ref[:, here] = jnp.dot(
            shell_ref[...], hot, preferred_element_type=jnp.float32
        ).astype(jnp.bfloat16)
        area = area_ref[here].reshape(1, span)
        area_rows_ref[here, :] = jnp.broadcast_to(area, (LANES, span)).T
        for at in range(span):
            row = step * span + at
            rows_ref[pl.ds(pl.multiple_of(row * lane_blocks, lane_blocks), lane_blocks), :] = (
                table_ref[pl.ds(fluid_ref[row] * lane_blocks, lane_blocks), :]
            )
        return carry

    lax.fori_loop(0, STEPS, gather, 0)
    area = area_rows_ref[...]
    wet = jnp.concatenate(
        [
            (rows_ref[pl.ds(block, slots, stride=lane_blocks), :] * area).astype(jnp.bfloat16)
            for block in range(lane_blocks)
        ],
        1,
    )
    total = jnp.dot(pick_ref[...], wet, preferred_element_type=jnp.float32)
    pack(total[:, :cavity], part_ref)

    size = mine_ref.shape[0]
    own = rank_of(digits, PLANE)

    def rows_of(rank):
        return pl.ds(pl.multiple_of(rank * size, size), size)

    pl.semaphore_wait(barrier, len(plane) + len(stack))
    for slot, offset in enumerate(plane):
        there = moved(digits, PLANE, offset)
        pltpu.make_async_remote_copy(
            src_ref=part_ref.at[rows_of(rank_of(there, PLANE))],
            dst_ref=plane_ref.at[slot],
            send_sem=send_sem.at[0],
            recv_sem=recv_sem.at[0],
            device_id=place_of(there),
            device_id_type=MESH,
        ).start()

    shell_freq, shell_loss, cavity_freq, cavity_loss, freqs, force, source = [
        term[...].reshape(1, term.shape[0]) for term in terms
    ]
    frequencies = column_of(freqs)
    squared = frequencies * frequencies
    shell_p, shell_q = inverse_terms(shell_freq, shell_loss, squared)
    cavity_p, cavity_q = inverse_terms(cavity_freq, cavity_loss, squared)
    base_re = source * cavity_p
    base_im = -source * cavity_q
    back_p, back_q = squared * cavity_p, squared * cavity_q

    pltpu.make_async_copy(plane_ref, plane_ref, recv_sem.at[0]).wait()
    mine_ref[...] = (
        part_ref[rows_of(own), :].astype(jnp.float32)
        + jnp.sum(plane_ref[...].astype(jnp.float32), axis=0)
    ).astype(jnp.bfloat16)

    for slot, offset in enumerate(stack):
        pltpu.make_async_remote_copy(
            src_ref=mine_ref,
            dst_ref=stack_ref.at[slot],
            send_sem=send_sem.at[1],
            recv_sem=recv_sem.at[1],
            device_id=place_of(moved(digits, STACK, offset)),
            device_id_type=MESH,
        ).start()

    free = jnp.concatenate([base_re, base_im], 0).astype(jnp.bfloat16)
    for at in range(PARTS):
        here = pl.ds(at * (depth // PARTS), depth // PARTS)
        free_ref[:, here] = jnp.dot(free, modes_ref[:, here], preferred_element_type=jnp.float32)

    pltpu.make_async_copy(stack_ref, stack_ref, recv_sem.at[1]).wait()
    full_ref[rows_of(own), :] = (
        mine_ref[...].astype(jnp.float32)
        + jnp.sum(stack_ref[...].astype(jnp.float32), axis=0)
    ).astype(jnp.bfloat16)

    for offset in plane:
        pltpu.make_async_remote_copy(
            src_ref=full_ref.at[rows_of(own)],
            dst_ref=full_ref.at[rows_of(own)],
            send_sem=send_sem.at[2],
            recv_sem=recv_sem.at[2],
            device_id=place_of(moved(digits, PLANE, offset)),
            device_id_type=MESH,
        ).start()
    pltpu.make_async_copy(plane_ref, plane_ref, recv_sem.at[2]).wait()

    coupling = unpack(full_ref, shells, cavity)
    total_freqs = squared.shape[0]
    real, imag = base_re, base_im
    for section in range(SECTIONS):
        loads = lax.dot_general(
            jnp.concatenate([real, imag], 0).astype(jnp.bfloat16),
            coupling,
            (((1,), (1,)), ((), ())),
            preferred_element_type=jnp.float32,
        )
        load_re, load_im = force + loads[:total_freqs], loads[total_freqs:]
        struct_re = load_re * shell_p + load_im * shell_q
        struct_im = load_im * shell_p - load_re * shell_q
        back = jnp.dot(
            jnp.concatenate([struct_re, struct_im], 0).astype(jnp.bfloat16),
            coupling,
            preferred_element_type=jnp.float32,
        )
        back_re, back_im = back[:total_freqs], back[total_freqs:]
        coupled_re = back_re * back_p + back_im * back_q
        coupled_im = back_im * back_p - back_re * back_q
        real, imag = base_re + coupled_re, base_im + coupled_im
    amps_ref[pl.ds(0, total_freqs), :] = coupled_re.astype(jnp.bfloat16)
    amps_ref[pl.ds(total_freqs, total_freqs), :] = coupled_im.astype(jnp.bfloat16)
    structure_ref[0] = struct_re
    structure_ref[1] = struct_im

    pltpu.make_async_copy(plane_ref, plane_ref, send_sem.at[0]).wait()
    pltpu.make_async_copy(stack_ref, stack_ref, send_sem.at[1]).wait()
    pltpu.make_async_copy(plane_ref, plane_ref, send_sem.at[2]).wait()


def amplitudes(modes, shell, count, fluid_nodes, shell_nodes, area, terms, total_freqs):
    cavity, depth = modes.shape
    shells = shell.shape[0]
    slots = fluid_nodes.shape[0]
    planes, stacks = len(offsets_of(PLANE)), len(offsets_of(STACK))
    rows = rows_needed(shells, cavity, planes + 1)
    size = rows // (planes + 1)
    lane_blocks = pl.cdiv(cavity, LANES)
    outside = pl.BlockSpec(memory_space=pltpu.HBM)
    inside = pl.BlockSpec(memory_space=pltpu.VMEM)
    return pl.pallas_call(
        main_kernel,
        in_specs=[outside] * 2
        + [pl.BlockSpec(memory_space=pltpu.SMEM)]
        + [outside] * (3 + len(terms)),
        out_specs=[inside] * 4,
        out_shape=[
            jax.ShapeDtypeStruct((2 * total_freqs, cavity), jnp.bfloat16),
            jax.ShapeDtypeStruct((2, total_freqs, shells), jnp.float32),
            jax.ShapeDtypeStruct(modes.shape, modes.dtype),
            jax.ShapeDtypeStruct((2 * total_freqs, depth), jnp.float32),
        ],
        scratch_shapes=[
            pltpu.VMEM(shell.shape, shell.dtype),
            pltpu.SMEM((slots,), jnp.int32),
            pltpu.VMEM((slots,), jnp.int32),
            pltpu.VMEM((slots,), jnp.float32),
        ]
        + [pltpu.VMEM(term.shape, term.dtype) for term in terms]
        + [
            pltpu.VMEM((depth * lane_blocks, LANES), jnp.float32),
            pltpu.VMEM((slots * lane_blocks, LANES), jnp.float32),
            pltpu.VMEM((shells, slots), jnp.bfloat16),
            pltpu.VMEM((slots, LANES), jnp.float32),
            pltpu.VMEM((rows, LANES), jnp.bfloat16),
            pltpu.VMEM((planes, size, LANES), jnp.bfloat16),
            pltpu.VMEM((size, LANES), jnp.bfloat16),
            pltpu.VMEM((stacks, size, LANES), jnp.bfloat16),
            pltpu.VMEM((rows, LANES), jnp.bfloat16),
            pltpu.SemaphoreType.DMA((CHUNKS,)),
            pltpu.SemaphoreType.DMA((4 + len(terms),)),
            pltpu.SemaphoreType.DMA((3,)),
            pltpu.SemaphoreType.DMA((3,)),
        ],
        compiler_params=pltpu.CompilerParams(
            collective_id=0, has_side_effects=True, vmem_limit_bytes=34 << 20
        ),
    )(
        outer(modes),
        outer(shell),
        count,
        *[outer(value) for value in (fluid_nodes, shell_nodes, area, *terms)],
    )


def field_kernel(
    amps_ref, modes_ref, free_ref, structure_ref, pressure_hbm, own_hbm, held_ref, out_sem
):
    chunk = held_ref.shape[1]
    count = own_hbm.shape[1]
    first = pl.multiple_of(lax.axis_index("grp") * count, count)
    copies = [
        pltpu.make_async_copy(
            structure_ref.at[:, pl.ds(first, count), :], own_hbm, out_sem.at[held_ref.shape[0]]
        )
    ]
    copies[0].start()
    for at in range(held_ref.shape[0]):
        here = pl.ds(at * chunk, chunk)
        coupled = jnp.dot(
            amps_ref[...], modes_ref[:, here], preferred_element_type=jnp.float32
        )
        held_ref[at] = (free_ref[:, here] + coupled).T.astype(jnp.bfloat16)
        copies.append(
            pltpu.make_async_copy(held_ref.at[at], pressure_hbm.at[here], out_sem.at[at])
        )
        copies[-1].start()
    for copy in copies:
        copy.wait()


def field(amps, modes, free, structure, groups):
    depth = modes.shape[1]
    parts, count, shells = structure.shape
    half = amps.shape[0]
    inside = pl.BlockSpec(memory_space=pltpu.VMEM)
    return pl.pallas_call(
        field_kernel,
        in_specs=[inside] * 4,
        out_specs=[pl.BlockSpec(memory_space=pltpu.HBM)] * 2,
        out_shape=[
            jax.ShapeDtypeStruct((depth, half), jnp.bfloat16),
            jax.ShapeDtypeStruct((parts, count // groups, shells), jnp.float32),
        ],
        scratch_shapes=[
            pltpu.VMEM((PARTS, depth // PARTS, half), jnp.bfloat16),
            pltpu.SemaphoreType.DMA((PARTS + 1,)),
        ],
        compiler_params=pltpu.CompilerParams(vmem_limit_bytes=16 << 20),
    )(amps, modes, free, structure)


def on_device(acoustic_modes, shell_modes, wet_counts, fluid_nodes, shell_nodes, wet_area, *terms):
    amps, structure, modes, free = amplitudes(
        acoustic_modes.T,
        shell_modes.T,
        wet_counts,
        fluid_nodes,
        shell_nodes,
        wet_area,
        terms,
        terms[4].shape[0],
    )
    return tuple(field(amps, modes, free, structure, lax.axis_size("grp")))


def solution(mesh):
    both = P(("fluid", "grp"))
    placed = (P(("fluid", "grp"), None), P("fluid", None)) + (both,) * 4 + (P(),) * 7
    return jax.shard_map(
        on_device,
        mesh=mesh,
        in_specs=placed,
        out_specs=(P(("fluid", "grp"), None), P(None, "grp", None)),
        check_vma=False,
    )
```

```python
import jax
import jax.numpy as jnp
from jax import lax
from jax.experimental import pallas as pl
from jax.experimental.pallas import tpu as pltpu
from jax.sharding import PartitionSpec as P

SECTIONS = 4
MESH = pl.DeviceIdType.MESH
LANES = 128
SIZES = {"z": 8, "xh": 2, "y": 4, "xl": 2, "c": 2}
PLANE = ("xh", "y", "xl", "c")
STACK = ("z",)
CHUNKS = 4
PARTS = 8
STEPS = 4
TAIL = 4


def offsets_of(names):
    places = [()]
    for name in names:
        places = [place + (step,) for place in places for step in range(SIZES[name])]
    return sorted(places[1:], key=lambda place: (-hops(names, place), place[-1]))


def hops(names, place):
    return sum(
        min(step, SIZES[name] - step) for name, step in zip(names, place) if name != "c"
    )


def own_digits():
    fluid, grp = lax.axis_index("fluid"), lax.axis_index("grp")
    digits = {
        "z": fluid // 8,
        "xh": (fluid // 4) % 2,
        "y": fluid % 4,
        "xl": grp // 2,
        "c": grp % 2,
    }
    for name, size in SIZES.items():
        for step in range(1, size):
            digits[name, step] = lax.rem(digits[name] + step, size)
    return digits


def moved(digits, names, offset):
    there = dict(digits)
    for name, step in zip(names, offset):
        if step:
            there[name] = digits[name, step]
    return there


def place_of(digits):
    return (digits["z"] * 8 + digits["xh"] * 4 + digits["y"], digits["xl"] * 2 + digits["c"])


def rank_of(digits, names):
    rank = 0
    for name in names:
        rank = rank * SIZES[name] + digits[name]
    return rank


def column_of(row):
    size = row.shape[1]
    below = lax.broadcasted_iota(jnp.int32, (size, size), 0)
    across = lax.broadcasted_iota(jnp.int32, (size, size), 1)
    spread = jnp.where(below == across, jnp.broadcast_to(row, (size, size)), 0.0)
    return jnp.sum(spread, axis=1, keepdims=True)


def inverse_terms(omega, loss, squared):
    stiff = omega * omega
    real_part = stiff - squared
    imag_part = jnp.broadcast_to(loss * stiff, real_part.shape)
    scale = real_part * real_part + imag_part * imag_part
    return real_part / scale, imag_part / scale


def pad_lanes(values, width):
    if values.shape[1] == width:
        return values
    rest = jnp.zeros((values.shape[0], width - values.shape[1]), values.dtype)
    return jnp.concatenate([values, rest], 1)


def pad_rows(values, height):
    if values.shape[0] == height:
        return values
    rest = jnp.zeros((height - values.shape[0], values.shape[1]), values.dtype)
    return jnp.concatenate([values, rest], 0)


def tail_height(shells):
    return pl.cdiv(pl.cdiv(shells, TAIL), 16) * 16


def rows_needed(shells, cavity, parts):
    high = pl.cdiv(shells, 16) * 16
    used = high * (cavity // LANES) + tail_height(shells)
    return pl.cdiv(used, 16 * parts) * 16 * parts


def pack(total, out_ref):
    shells, cavity = total.shape
    high = pl.cdiv(shells, 16) * 16
    full = cavity // LANES
    for at in range(full):
        piece = pad_rows(total[:, at * LANES : (at + 1) * LANES], high)
        out_ref[pl.ds(at * high, high), :] = piece.astype(out_ref.dtype)
    tall, wide = tail_height(shells), LANES // TAIL
    rest = pad_lanes(pad_rows(total[:, full * LANES :], tall * TAIL), wide)
    tail = jnp.concatenate([rest[at * tall : (at + 1) * tall] for at in range(TAIL)], 1)
    height = out_ref.shape[0] - full * high
    out_ref[pl.ds(full * high, height), :] = pad_rows(tail, height).astype(out_ref.dtype)


def unpack(full_ref, shells, cavity):
    high = pl.cdiv(shells, 16) * 16
    full = cavity // LANES
    tall, wide = tail_height(shells), LANES // TAIL
    blocks = [full_ref[pl.ds(at * high, high), :] for at in range(full)]
    tail = full_ref[pl.ds(full * high, tall), :].astype(jnp.float32)
    rest = [tail[:, at * wide : at * wide + cavity - full * LANES] for at in range(TAIL)]
    rest = jnp.concatenate(rest, 0)[:high].astype(full_ref.dtype)
    return jnp.concatenate(blocks + [rest], 1)[:shells]


def outer(value):
    return pltpu.with_memory_space_constraint(value, pltpu.HBM)


def main_kernel(
    modes_hbm,
    shell_hbm,
    count_ref,
    fluid_hbm,
    node_hbm,
    area_hbm,
    *rest,
):
    terms_hbm = rest[:7]
    amps_ref, structure_ref, modes_ref, free_ref = rest[7:11]
    shell_ref, fluid_ref, node_ref, area_ref = rest[11:15]
    terms = rest[15:22]
    table_ref, rows_ref, pick_ref, area_rows_ref = rest[22:26]
    part_ref, plane_ref, mine_ref, stack_ref, full_ref = rest[26:31]
    modes_sem, small_sem, send_sem, recv_sem = rest[31:]

    cavity, depth = modes_ref.shape
    shells, shell_depth = shell_ref.shape
    slots = fluid_ref.shape[0]
    chunk, span = depth // CHUNKS, slots // STEPS
    lane_blocks = pl.cdiv(cavity, LANES)

    small = [
        pltpu.make_async_copy(source, target, small_sem.at[at])
        for at, (source, target) in enumerate(
            [
                (shell_hbm, shell_ref),
                (node_hbm, node_ref),
                (area_hbm, area_ref),
                (fluid_hbm, fluid_ref),
            ]
            + list(zip(terms_hbm, terms))
        )
    ]
    large = [
        pltpu.make_async_copy(
            modes_hbm.at[:, pl.ds(at * chunk, chunk)],
            modes_ref.at[:, pl.ds(at * chunk, chunk)],
            modes_sem.at[at],
        )
        for at in range(CHUNKS)
    ]
    for copy in large[:1] + small + large[1:]:
        copy.start()

    digits = own_digits()
    plane, stack = offsets_of(PLANE), offsets_of(STACK)
    barrier = pltpu.get_barrier_semaphore()
    for names, offsets in ((PLANE, plane), (STACK, stack)):
        for offset in offsets:
            pl.semaphore_signal(
                barrier,
                inc=1,
                device_id=place_of(moved(digits, names, offset)),
                device_id_type=MESH,
            )

    for at in range(CHUNKS):
        large[at].wait()
        for block in range(lane_blocks):
            first = block * LANES
            wide = min(LANES, cavity - first)
            piece = modes_ref[first : first + wide, at * chunk : (at + 1) * chunk].T
            table_ref[pl.ds(at * chunk * lane_blocks + block, chunk, stride=lane_blocks), :] = (
                pad_lanes(piece.astype(jnp.float32), LANES)
            )
    for copy in small:
        copy.wait()
    count = count_ref[0]

    def gather(step, carry):
        here = pl.ds(pl.multiple_of(step * span, span), span)
        slot = lax.broadcasted_iota(jnp.int32, (1, span), 1) + step * span
        node = jnp.where(slot < count, node_ref[here].reshape(1, span), -1)
        number = lax.broadcasted_iota(jnp.int32, (shell_depth, span), 0)
        hot = jnp.where(number == node, 1.0, 0.0).astype(jnp.bfloat16)
        pick_ref[:, here] = jnp.dot(
            shell_ref[...], hot, preferred_element_type=jnp.float32
        ).astype(jnp.bfloat16)
        area = area_ref[here].reshape(1, span)
        area_rows_ref[here, :] = jnp.broadcast_to(area, (LANES, span)).T
        for at in range(span):
            row = step * span + at
            rows_ref[pl.ds(pl.multiple_of(row * lane_blocks, lane_blocks), lane_blocks), :] = (
                table_ref[pl.ds(fluid_ref[row] * lane_blocks, lane_blocks), :]
            )
        return carry

    lax.fori_loop(0, STEPS, gather, 0)
    area = area_rows_ref[...]
    wet = jnp.concatenate(
        [
            (rows_ref[pl.ds(block, slots, stride=lane_blocks), :] * area).astype(jnp.bfloat16)
            for block in range(lane_blocks)
        ],
        1,
    )
    total = jnp.dot(pick_ref[...], wet, preferred_element_type=jnp.float32)
    pack(total[:, :cavity], part_ref)

    size = mine_ref.shape[0]
    own = rank_of(digits, PLANE)

    def rows_of(rank):
        return pl.ds(pl.multiple_of(rank * size, size), size)

    pl.semaphore_wait(barrier, len(plane) + len(stack))
    for slot, offset in enumerate(plane):
        there = moved(digits, PLANE, offset)
        pltpu.make_async_remote_copy(
            src_ref=part_ref.at[rows_of(rank_of(there, PLANE))],
            dst_ref=plane_ref.at[slot],
            send_sem=send_sem.at[0],
            recv_sem=recv_sem.at[0],
            device_id=place_of(there),
            device_id_type=MESH,
        ).start()

    shell_freq, shell_loss, cavity_freq, cavity_loss, freqs, force, source = [
        term[...].reshape(1, term.shape[0]) for term in terms
    ]
    frequencies = column_of(freqs)
    squared = frequencies * frequencies
    shell_p, shell_q = inverse_terms(shell_freq, shell_loss, squared)
    cavity_p, cavity_q = inverse_terms(cavity_freq, cavity_loss, squared)
    base_re = source * cavity_p
    base_im = -source * cavity_q
    back_p, back_q = squared * cavity_p, squared * cavity_q

    pltpu.make_async_copy(plane_ref, plane_ref, recv_sem.at[0]).wait()
    mine_ref[...] = (
        part_ref[rows_of(own), :].astype(jnp.float32)
        + jnp.sum(plane_ref[...].astype(jnp.float32), axis=0)
    ).astype(jnp.bfloat16)

    for slot, offset in enumerate(stack):
        pltpu.make_async_remote_copy(
            src_ref=mine_ref,
            dst_ref=stack_ref.at[slot],
            send_sem=send_sem.at[1],
            recv_sem=recv_sem.at[1],
            device_id=place_of(moved(digits, STACK, offset)),
            device_id_type=MESH,
        ).start()

    free = jnp.concatenate([base_re, base_im], 0).astype(jnp.bfloat16)
    for at in range(PARTS):
        here = pl.ds(at * (depth // PARTS), depth // PARTS)
        free_ref[:, here] = jnp.dot(free, modes_ref[:, here], preferred_element_type=jnp.float32)

    pltpu.make_async_copy(stack_ref, stack_ref, recv_sem.at[1]).wait()
    full_ref[rows_of(own), :] = (
        mine_ref[...].astype(jnp.float32)
        + jnp.sum(stack_ref[...].astype(jnp.float32), axis=0)
    ).astype(jnp.bfloat16)

    for offset in plane:
        pltpu.make_async_remote_copy(
            src_ref=full_ref.at[rows_of(own)],
            dst_ref=full_ref.at[rows_of(own)],
            send_sem=send_sem.at[2],
            recv_sem=recv_sem.at[2],
            device_id=place_of(moved(digits, PLANE, offset)),
            device_id_type=MESH,
        ).start()
    pltpu.make_async_copy(plane_ref, plane_ref, recv_sem.at[2]).wait()

    coupling = unpack(full_ref, shells, cavity)
    total_freqs = squared.shape[0]
    real, imag = base_re, base_im
    for section in range(SECTIONS):
        loads = lax.dot_general(
            jnp.concatenate([real, imag], 0).astype(jnp.bfloat16),
            coupling,
            (((1,), (1,)), ((), ())),
            preferred_element_type=jnp.float32,
        )
        load_re, load_im = force + loads[:total_freqs], loads[total_freqs:]
        struct_re = load_re * shell_p + load_im * shell_q
        struct_im = load_im * shell_p - load_re * shell_q
        back = jnp.dot(
            jnp.concatenate([struct_re, struct_im], 0).astype(jnp.bfloat16),
            coupling,
            preferred_element_type=jnp.float32,
        )
        back_re, back_im = back[:total_freqs], back[total_freqs:]
        coupled_re = back_re * back_p + back_im * back_q
        coupled_im = back_im * back_p - back_re * back_q
        real, imag = base_re + coupled_re, base_im + coupled_im
    amps_ref[pl.ds(0, total_freqs), :] = coupled_re.astype(jnp.bfloat16)
    amps_ref[pl.ds(total_freqs, total_freqs), :] = coupled_im.astype(jnp.bfloat16)
    structure_ref[0] = struct_re
    structure_ref[1] = struct_im

    pltpu.make_async_copy(plane_ref, plane_ref, send_sem.at[0]).wait()
    pltpu.make_async_copy(stack_ref, stack_ref, send_sem.at[1]).wait()
    pltpu.make_async_copy(plane_ref, plane_ref, send_sem.at[2]).wait()


def amplitudes(modes, shell, count, fluid_nodes, shell_nodes, area, terms, total_freqs):
    cavity, depth = modes.shape
    shells = shell.shape[0]
    slots = fluid_nodes.shape[0]
    planes, stacks = len(offsets_of(PLANE)), len(offsets_of(STACK))
    rows = rows_needed(shells, cavity, planes + 1)
    size = rows // (planes + 1)
    lane_blocks = pl.cdiv(cavity, LANES)
    outside = pl.BlockSpec(memory_space=pltpu.HBM)
    inside = pl.BlockSpec(memory_space=pltpu.VMEM)
    return pl.pallas_call(
        main_kernel,
        in_specs=[outside] * 2
        + [pl.BlockSpec(memory_space=pltpu.SMEM)]
        + [outside] * (3 + len(terms)),
        out_specs=[inside] * 4,
        out_shape=[
            jax.ShapeDtypeStruct((2 * total_freqs, cavity), jnp.bfloat16),
            jax.ShapeDtypeStruct((2, total_freqs, shells), jnp.float32),
            jax.ShapeDtypeStruct(modes.shape, modes.dtype),
            jax.ShapeDtypeStruct((2 * total_freqs, depth), jnp.float32),
        ],
        scratch_shapes=[
            pltpu.VMEM(shell.shape, shell.dtype),
            pltpu.SMEM((slots,), jnp.int32),
            pltpu.VMEM((slots,), jnp.int32),
            pltpu.VMEM((slots,), jnp.float32),
        ]
        + [pltpu.VMEM(term.shape, term.dtype) for term in terms]
        + [
            pltpu.VMEM((depth * lane_blocks, LANES), jnp.float32),
            pltpu.VMEM((slots * lane_blocks, LANES), jnp.float32),
            pltpu.VMEM((shells, slots), jnp.bfloat16),
            pltpu.VMEM((slots, LANES), jnp.float32),
            pltpu.VMEM((rows, LANES), jnp.bfloat16),
            pltpu.VMEM((planes, size, LANES), jnp.bfloat16),
            pltpu.VMEM((size, LANES), jnp.bfloat16),
            pltpu.VMEM((stacks, size, LANES), jnp.bfloat16),
            pltpu.VMEM((rows, LANES), jnp.bfloat16),
            pltpu.SemaphoreType.DMA((CHUNKS,)),
            pltpu.SemaphoreType.DMA((4 + len(terms),)),
            pltpu.SemaphoreType.DMA((3,)),
            pltpu.SemaphoreType.DMA((3,)),
        ],
        compiler_params=pltpu.CompilerParams(
            collective_id=0, has_side_effects=True, vmem_limit_bytes=34 << 20
        ),
    )(
        outer(modes),
        outer(shell),
        count,
        *[outer(value) for value in (fluid_nodes, shell_nodes, area, *terms)],
    )


def field_kernel(
    amps_ref, modes_ref, free_ref, structure_ref, pressure_hbm, own_hbm, held_ref, out_sem
):
    chunk = held_ref.shape[1]
    count = own_hbm.shape[1]
    first = pl.multiple_of(lax.axis_index("grp") * count, count)
    copies = [
        pltpu.make_async_copy(
            structure_ref.at[:, pl.ds(first, count), :], own_hbm, out_sem.at[held_ref.shape[0]]
        )
    ]
    copies[0].start()
    for at in range(held_ref.shape[0]):
        here = pl.ds(at * chunk, chunk)
        coupled = jnp.dot(
            amps_ref[...], modes_ref[:, here], preferred_element_type=jnp.float32
        )
        held_ref[at] = (free_ref[:, here] + coupled).T.astype(jnp.bfloat16)
        copies.append(
            pltpu.make_async_copy(held_ref.at[at], pressure_hbm.at[here], out_sem.at[at])
        )
        copies[-1].start()
    for copy in copies:
        copy.wait()


def field(amps, modes, free, structure, groups):
    depth = modes.shape[1]
    parts, count, shells = structure.shape
    half = amps.shape[0]
    inside = pl.BlockSpec(memory_space=pltpu.VMEM)
    return pl.pallas_call(
        field_kernel,
        in_specs=[inside] * 4,
        out_specs=[pl.BlockSpec(memory_space=pltpu.HBM)] * 2,
        out_shape=[
            jax.ShapeDtypeStruct((depth, half), jnp.bfloat16),
            jax.ShapeDtypeStruct((parts, count // groups, shells), jnp.float32),
        ],
        scratch_shapes=[
            pltpu.VMEM((PARTS, depth // PARTS, half), jnp.bfloat16),
            pltpu.SemaphoreType.DMA((PARTS + 1,)),
        ],
        compiler_params=pltpu.CompilerParams(vmem_limit_bytes=16 << 20),
    )(amps, modes, free, structure)


def on_device(acoustic_modes, shell_modes, wet_counts, fluid_nodes, shell_nodes, wet_area, *terms):
    amps, structure, modes, free = amplitudes(
        acoustic_modes.T,
        shell_modes.T,
        wet_counts,
        fluid_nodes,
        shell_nodes,
        wet_area,
        terms,
        terms[4].shape[0],
    )
    return tuple(field(amps, modes, free, structure, lax.axis_size("grp")))


def solution(mesh):
    both = P(("fluid", "grp"))
    placed = (P(("fluid", "grp"), None), P("fluid", None)) + (both,) * 4 + (P(),) * 7
    return jax.shard_map(
        on_device,
        mesh=mesh,
        in_specs=placed,
        out_specs=(P(("fluid", "grp"), None), P(None, "grp", None)),
        check_vma=False,
    )
```

```python
import jax
import jax.numpy as jnp
from jax import lax
from jax.experimental import pallas as pl
from jax.experimental.pallas import tpu as pltpu
from jax.sharding import PartitionSpec as P

SECTIONS = 4
MESH = pl.DeviceIdType.MESH
LANES = 128
SIZES = {"z": 8, "xh": 2, "y": 4, "xl": 2, "c": 2}
PLANE = ("xh", "y", "xl", "c")
STACK = ("z",)
CHUNKS = 4
PARTS = 8
STEPS = 8
TAIL = 4


def offsets_of(names):
    places = [()]
    for name in names:
        places = [place + (step,) for place in places for step in range(SIZES[name])]
    return sorted(places[1:], key=lambda place: (-hops(names, place), place[-1]))


def hops(names, place):
    return sum(
        min(step, SIZES[name] - step) for name, step in zip(names, place) if name != "c"
    )


def own_digits():
    fluid, grp = lax.axis_index("fluid"), lax.axis_index("grp")
    digits = {
        "z": fluid // 8,
        "xh": (fluid // 4) % 2,
        "y": fluid % 4,
        "xl": grp // 2,
        "c": grp % 2,
    }
    for name, size in SIZES.items():
        for step in range(1, size):
            digits[name, step] = lax.rem(digits[name] + step, size)
    return digits


def moved(digits, names, offset):
    there = dict(digits)
    for name, step in zip(names, offset):
        if step:
            there[name] = digits[name, step]
    return there


def place_of(digits):
    return (digits["z"] * 8 + digits["xh"] * 4 + digits["y"], digits["xl"] * 2 + digits["c"])


def rank_of(digits, names):
    rank = 0
    for name in names:
        rank = rank * SIZES[name] + digits[name]
    return rank


def column_of(row):
    size = row.shape[1]
    below = lax.broadcasted_iota(jnp.int32, (size, size), 0)
    across = lax.broadcasted_iota(jnp.int32, (size, size), 1)
    spread = jnp.where(below == across, jnp.broadcast_to(row, (size, size)), 0.0)
    return jnp.sum(spread, axis=1, keepdims=True)


def inverse_terms(omega, loss, squared):
    stiff = omega * omega
    real_part = stiff - squared
    imag_part = jnp.broadcast_to(loss * stiff, real_part.shape)
    scale = real_part * real_part + imag_part * imag_part
    return real_part / scale, imag_part / scale


def pad_lanes(values, width):
    if values.shape[1] == width:
        return values
    rest = jnp.zeros((values.shape[0], width - values.shape[1]), values.dtype)
    return jnp.concatenate([values, rest], 1)


def pad_rows(values, height):
    if values.shape[0] == height:
        return values
    rest = jnp.zeros((height - values.shape[0], values.shape[1]), values.dtype)
    return jnp.concatenate([values, rest], 0)


def tail_height(shells):
    return pl.cdiv(pl.cdiv(shells, TAIL), 16) * 16


def rows_needed(shells, cavity, parts):
    high = pl.cdiv(shells, 16) * 16
    used = high * (cavity // LANES) + tail_height(shells)
    return pl.cdiv(used, 16 * parts) * 16 * parts


def pack(total, out_ref):
    shells, cavity = total.shape
    high = pl.cdiv(shells, 16) * 16
    full = cavity // LANES
    for at in range(full):
        piece = pad_rows(total[:, at * LANES : (at + 1) * LANES], high)
        out_ref[pl.ds(at * high, high), :] = piece.astype(out_ref.dtype)
    tall, wide = tail_height(shells), LANES // TAIL
    rest = pad_lanes(pad_rows(total[:, full * LANES :], tall * TAIL), wide)
    tail = jnp.concatenate([rest[at * tall : (at + 1) * tall] for at in range(TAIL)], 1)
    height = out_ref.shape[0] - full * high
    out_ref[pl.ds(full * high, height), :] = pad_rows(tail, height).astype(out_ref.dtype)


def unpack(full_ref, shells, cavity):
    high = pl.cdiv(shells, 16) * 16
    full = cavity // LANES
    tall, wide = tail_height(shells), LANES // TAIL
    blocks = [full_ref[pl.ds(at * high, high), :] for at in range(full)]
    tail = full_ref[pl.ds(full * high, tall), :].astype(jnp.float32)
    rest = [tail[:, at * wide : at * wide + cavity - full * LANES] for at in range(TAIL)]
    rest = jnp.concatenate(rest, 0)[:high].astype(full_ref.dtype)
    return jnp.concatenate(blocks + [rest], 1)[:shells]


def outer(value):
    return pltpu.with_memory_space_constraint(value, pltpu.HBM)


def main_kernel(
    modes_hbm,
    shell_hbm,
    count_ref,
    fluid_hbm,
    node_hbm,
    area_hbm,
    *rest,
):
    terms_hbm = rest[:7]
    amps_ref, structure_ref, modes_ref, free_ref = rest[7:11]
    shell_ref, fluid_ref, node_ref, area_ref = rest[11:15]
    terms = rest[15:22]
    table_ref, total_ref = rest[22:24]
    part_ref, plane_ref, mine_ref, stack_ref, full_ref = rest[24:29]
    modes_sem, small_sem, send_sem, recv_sem = rest[29:33]
    rows, picks = rest[33 : 33 + STEPS], rest[33 + STEPS :]

    cavity, depth = modes_ref.shape
    shells, shell_depth = shell_ref.shape
    slots = fluid_ref.shape[0]
    chunk, span = depth // CHUNKS, slots // STEPS
    lane_blocks = pl.cdiv(cavity, LANES)

    small = [
        pltpu.make_async_copy(source, target, small_sem.at[at])
        for at, (source, target) in enumerate(
            [
                (shell_hbm, shell_ref),
                (node_hbm, node_ref),
                (area_hbm, area_ref),
                (fluid_hbm, fluid_ref),
            ]
            + list(zip(terms_hbm, terms))
        )
    ]
    large = [
        pltpu.make_async_copy(
            modes_hbm.at[:, pl.ds(at * chunk, chunk)],
            modes_ref.at[:, pl.ds(at * chunk, chunk)],
            modes_sem.at[at],
        )
        for at in range(CHUNKS)
    ]
    for copy in large[:1] + small + large[1:]:
        copy.start()

    digits = own_digits()
    plane, stack = offsets_of(PLANE), offsets_of(STACK)
    barrier = pltpu.get_barrier_semaphore()
    for names, offsets in ((PLANE, plane), (STACK, stack)):
        for offset in offsets:
            pl.semaphore_signal(
                barrier,
                inc=1,
                device_id=place_of(moved(digits, names, offset)),
                device_id_type=MESH,
            )

    for at in range(CHUNKS):
        large[at].wait()
        for block in range(lane_blocks):
            first = block * LANES
            wide = min(LANES, cavity - first)
            piece = modes_ref[first : first + wide, at * chunk : (at + 1) * chunk].T
            table_ref[pl.ds(at * chunk * lane_blocks + block, chunk, stride=lane_blocks), :] = (
                pad_lanes(piece.astype(jnp.float32), LANES)
            )
    for copy in small:
        copy.wait()
    count = count_ref[0]

    for step in range(STEPS):
        slot = lax.broadcasted_iota(jnp.int32, (1, span), 1) + step * span
        here = pl.ds(step * span, span)
        node = jnp.where(slot < count, node_ref[here].reshape(1, span), -1)
        number = lax.broadcasted_iota(jnp.int32, (shell_depth, span), 0)
        hot = jnp.where(number == node, 1.0, 0.0).astype(jnp.bfloat16)
        picks[step][...] = jnp.dot(
            shell_ref[...], hot, preferred_element_type=jnp.float32
        ).astype(jnp.bfloat16)
        for at in range(span):
            rows[step][pl.ds(at * lane_blocks, lane_blocks), :] = table_ref[
                pl.ds(fluid_ref[step * span + at] * lane_blocks, lane_blocks), :
            ]
        area = jnp.broadcast_to(area_ref[here].reshape(1, span), (LANES, span)).T
        wet = jnp.concatenate(
            [
                (rows[step][pl.ds(block, span, stride=lane_blocks), :] * area).astype(
                    jnp.bfloat16
                )
                for block in range(lane_blocks)
            ],
            1,
        )
        product = jnp.dot(picks[step][...], wet, preferred_element_type=jnp.float32)
        total_ref[...] = product if step == 0 else total_ref[...] + product
    total = total_ref[...]
    pack(total[:, :cavity], part_ref)

    size = mine_ref.shape[0]
    own = rank_of(digits, PLANE)

    def rows_of(rank):
        return pl.ds(pl.multiple_of(rank * size, size), size)

    pl.semaphore_wait(barrier, len(plane) + len(stack))
    for slot, offset in enumerate(plane):
        there = moved(digits, PLANE, offset)
        pltpu.make_async_remote_copy(
            src_ref=part_ref.at[rows_of(rank_of(there, PLANE))],
            dst_ref=plane_ref.at[slot],
            send_sem=send_sem.at[0],
            recv_sem=recv_sem.at[0],
            device_id=place_of(there),
            device_id_type=MESH,
        ).start()

    shell_freq, shell_loss, cavity_freq, cavity_loss, freqs, force, source = [
        term[...].reshape(1, term.shape[0]) for term in terms
    ]
    frequencies = column_of(freqs)
    squared = frequencies * frequencies
    shell_p, shell_q = inverse_terms(shell_freq, shell_loss, squared)
    cavity_p, cavity_q = inverse_terms(cavity_freq, cavity_loss, squared)
    base_re = source * cavity_p
    base_im = -source * cavity_q
    back_p, back_q = squared * cavity_p, squared * cavity_q

    pltpu.make_async_copy(plane_ref, plane_ref, recv_sem.at[0]).wait()
    mine_ref[...] = (
        part_ref[rows_of(own), :].astype(jnp.float32)
        + jnp.sum(plane_ref[...].astype(jnp.float32), axis=0)
    ).astype(jnp.bfloat16)

    for slot, offset in enumerate(stack):
        pltpu.make_async_remote_copy(
            src_ref=mine_ref,
            dst_ref=stack_ref.at[slot],
            send_sem=send_sem.at[1],
            recv_sem=recv_sem.at[1],
            device_id=place_of(moved(digits, STACK, offset)),
            device_id_type=MESH,
        ).start()

    free = jnp.concatenate([base_re, base_im], 0).astype(jnp.bfloat16)
    for at in range(PARTS):
        here = pl.ds(at * (depth // PARTS), depth // PARTS)
        free_ref[:, here] = jnp.dot(free, modes_ref[:, here], preferred_element_type=jnp.float32)

    pltpu.make_async_copy(stack_ref, stack_ref, recv_sem.at[1]).wait()
    full_ref[rows_of(own), :] = (
        mine_ref[...].astype(jnp.float32)
        + jnp.sum(stack_ref[...].astype(jnp.float32), axis=0)
    ).astype(jnp.bfloat16)

    for offset in plane:
        pltpu.make_async_remote_copy(
            src_ref=full_ref.at[rows_of(own)],
            dst_ref=full_ref.at[rows_of(own)],
            send_sem=send_sem.at[2],
            recv_sem=recv_sem.at[2],
            device_id=place_of(moved(digits, PLANE, offset)),
            device_id_type=MESH,
        ).start()
    pltpu.make_async_copy(plane_ref, plane_ref, recv_sem.at[2]).wait()

    coupling = unpack(full_ref, shells, cavity)
    total_freqs = squared.shape[0]
    real, imag = base_re, base_im
    for section in range(SECTIONS):
        loads = lax.dot_general(
            jnp.concatenate([real, imag], 0).astype(jnp.bfloat16),
            coupling,
            (((1,), (1,)), ((), ())),
            preferred_element_type=jnp.float32,
        )
        load_re, load_im = force + loads[:total_freqs], loads[total_freqs:]
        struct_re = load_re * shell_p + load_im * shell_q
        struct_im = load_im * shell_p - load_re * shell_q
        back = jnp.dot(
            jnp.concatenate([struct_re, struct_im], 0).astype(jnp.bfloat16),
            coupling,
            preferred_element_type=jnp.float32,
        )
        back_re, back_im = back[:total_freqs], back[total_freqs:]
        coupled_re = back_re * back_p + back_im * back_q
        coupled_im = back_im * back_p - back_re * back_q
        real, imag = base_re + coupled_re, base_im + coupled_im
    amps_ref[pl.ds(0, total_freqs), :] = coupled_re.astype(jnp.bfloat16)
    amps_ref[pl.ds(total_freqs, total_freqs), :] = coupled_im.astype(jnp.bfloat16)
    structure_ref[0] = struct_re
    structure_ref[1] = struct_im

    pltpu.make_async_copy(plane_ref, plane_ref, send_sem.at[0]).wait()
    pltpu.make_async_copy(stack_ref, stack_ref, send_sem.at[1]).wait()
    pltpu.make_async_copy(plane_ref, plane_ref, send_sem.at[2]).wait()


def amplitudes(modes, shell, count, fluid_nodes, shell_nodes, area, terms, total_freqs):
    cavity, depth = modes.shape
    shells = shell.shape[0]
    slots = fluid_nodes.shape[0]
    planes, stacks = len(offsets_of(PLANE)), len(offsets_of(STACK))
    rows = rows_needed(shells, cavity, planes + 1)
    size = rows // (planes + 1)
    lane_blocks = pl.cdiv(cavity, LANES)
    outside = pl.BlockSpec(memory_space=pltpu.HBM)
    inside = pl.BlockSpec(memory_space=pltpu.VMEM)
    return pl.pallas_call(
        main_kernel,
        in_specs=[outside] * 2
        + [pl.BlockSpec(memory_space=pltpu.SMEM)]
        + [outside] * (3 + len(terms)),
        out_specs=[inside] * 4,
        out_shape=[
            jax.ShapeDtypeStruct((2 * total_freqs, cavity), jnp.bfloat16),
            jax.ShapeDtypeStruct((2, total_freqs, shells), jnp.float32),
            jax.ShapeDtypeStruct(modes.shape, modes.dtype),
            jax.ShapeDtypeStruct((2 * total_freqs, depth), jnp.float32),
        ],
        scratch_shapes=[
            pltpu.VMEM(shell.shape, shell.dtype),
            pltpu.SMEM((slots,), jnp.int32),
            pltpu.VMEM((slots,), jnp.int32),
            pltpu.VMEM((slots,), jnp.float32),
        ]
        + [pltpu.VMEM(term.shape, term.dtype) for term in terms]
        + [
            pltpu.VMEM((depth * lane_blocks, LANES), jnp.float32),
            pltpu.VMEM((shells, lane_blocks * LANES), jnp.float32),
            pltpu.VMEM((rows, LANES), jnp.bfloat16),
            pltpu.VMEM((planes, size, LANES), jnp.bfloat16),
            pltpu.VMEM((size, LANES), jnp.bfloat16),
            pltpu.VMEM((stacks, size, LANES), jnp.bfloat16),
            pltpu.VMEM((rows, LANES), jnp.bfloat16),
            pltpu.SemaphoreType.DMA((CHUNKS,)),
            pltpu.SemaphoreType.DMA((4 + len(terms),)),
            pltpu.SemaphoreType.DMA((3,)),
            pltpu.SemaphoreType.DMA((3,)),
        ]
        + [pltpu.VMEM((slots // STEPS * lane_blocks, LANES), jnp.float32)] * STEPS
        + [pltpu.VMEM((shells, slots // STEPS), jnp.bfloat16)] * STEPS,
        compiler_params=pltpu.CompilerParams(
            collective_id=0, has_side_effects=True, vmem_limit_bytes=34 << 20
        ),
    )(
        outer(modes),
        outer(shell),
        count,
        *[outer(value) for value in (fluid_nodes, shell_nodes, area, *terms)],
    )


def field_kernel(
    amps_ref, modes_ref, free_ref, structure_ref, pressure_hbm, own_hbm, held_ref, out_sem
):
    chunk = held_ref.shape[1]
    count = own_hbm.shape[1]
    first = pl.multiple_of(lax.axis_index("grp") * count, count)
    copies = [
        pltpu.make_async_copy(
            structure_ref.at[:, pl.ds(first, count), :], own_hbm, out_sem.at[held_ref.shape[0]]
        )
    ]
    copies[0].start()
    for at in range(held_ref.shape[0]):
        here = pl.ds(at * chunk, chunk)
        coupled = jnp.dot(
            amps_ref[...], modes_ref[:, here], preferred_element_type=jnp.float32
        )
        held_ref[at] = (free_ref[:, here] + coupled).T.astype(jnp.bfloat16)
        copies.append(
            pltpu.make_async_copy(held_ref.at[at], pressure_hbm.at[here], out_sem.at[at])
        )
        copies[-1].start()
    for copy in copies:
        copy.wait()


def field(amps, modes, free, structure, groups):
    depth = modes.shape[1]
    parts, count, shells = structure.shape
    half = amps.shape[0]
    inside = pl.BlockSpec(memory_space=pltpu.VMEM)
    return pl.pallas_call(
        field_kernel,
        in_specs=[inside] * 4,
        out_specs=[pl.BlockSpec(memory_space=pltpu.HBM)] * 2,
        out_shape=[
            jax.ShapeDtypeStruct((depth, half), jnp.bfloat16),
            jax.ShapeDtypeStruct((parts, count // groups, shells), jnp.float32),
        ],
        scratch_shapes=[
            pltpu.VMEM((PARTS, depth // PARTS, half), jnp.bfloat16),
            pltpu.SemaphoreType.DMA((PARTS + 1,)),
        ],
        compiler_params=pltpu.CompilerParams(vmem_limit_bytes=16 << 20),
    )(amps, modes, free, structure)


def on_device(acoustic_modes, shell_modes, wet_counts, fluid_nodes, shell_nodes, wet_area, *terms):
    amps, structure, modes, free = amplitudes(
        acoustic_modes.T,
        shell_modes.T,
        wet_counts,
        fluid_nodes,
        shell_nodes,
        wet_area,
        terms,
        terms[4].shape[0],
    )
    return tuple(field(amps, modes, free, structure, lax.axis_size("grp")))


def solution(mesh):
    both = P(("fluid", "grp"))
    placed = (P(("fluid", "grp"), None), P("fluid", None)) + (both,) * 4 + (P(),) * 7
    return jax.shard_map(
        on_device,
        mesh=mesh,
        in_specs=placed,
        out_specs=(P(("fluid", "grp"), None), P(None, "grp", None)),
        check_vma=False,
    )
```
